512 devices in a mesh: ch: 64 (over z_hi, y, core), freq: 8 (over z_lo, x).
Axes of the slice: x: 4, y: 8, z: 8 (z_hi: 4, z_lo: 2; z = z_hi * 2 + z_lo), core: 2. Of those that a mesh axis runs over, the one named last changes fastest.
Arguments:
- strain: bfloat16 [2048, 8, 2048], P('ch'), may hold values from -100 to 100
- channel_ok: int32 [2048], P('ch'), may hold values 0 or 1
- window_ok: int32 [2048, 8], P('ch'), may hold values 0 or 1
Outputs:
- stack_ahead: bfloat16 [2, 256, 2048, 128], P(None, 'freq', 'ch')
- stack_behind: bfloat16 [2, 256, 2048, 128], P(None, 'freq', 'ch')
The draws below stay inside these ranges and needn't reach their ends.
All inputs are finite; a program needn't handle non-finite values. No bound on the sum of `channel_ok` or of `window_ok` on one device may be relied on, other than what follows from the above.
Results may differ from the reference program's by a relative error of at most 0.0082.
Values may be sent and summed in bfloat16 or wider, within the bound.
A program may use at most 64 MiB of HBM per device.

```python
import math
import jax
import jax.numpy as jnp
from jax import lax

WINDOWS = 8
SAMPLES = 2048
BINS = 256
REACH = 128
TIME_HALF = 128
BIN_HALF = 32
CHANNELS = 2048


def draw_strain(key, part):
    key_list = jax.random.split(jax.random.fold_in(key, 11), 4)
    segments = SAMPLES // 64
    shape_full = (CHANNELS, WINDOWS, SAMPLES)
    base_noise = jnp.clip(jax.random.normal(key_list[0], shape_full, jnp.float32), -4.0, 4.0)
    channel_gain = jnp.exp(jax.random.uniform(key_list[2], (CHANNELS, 1, 1), jnp.float32, 0.0, math.log(10.0)))
    envelope = jnp.exp(jax.random.uniform(key_list[3], (CHANNELS, WINDOWS, segments), jnp.float32, math.log(0.3), math.log(3.0)))
    result = base_noise * channel_gain * jnp.repeat(envelope, 64, axis=2)
    return jnp.clip(result, -100.0, 100.0).astype(jnp.bfloat16)


def place_ends(values, rng, least, largest):
    longest = values.shape.index(max(values.shape))
    spots = []
    for shift in (0, 1):
        where = [jax.random.randint(jax.random.fold_in(rng, axis), (), 0, length) for axis, length in enumerate(values.shape)]
        where[longest] = (where[longest] + shift) % values.shape[longest]
        spots.append(tuple(where))
    return values.at[spots[0]].set(least).at[spots[1]].set(largest)


def setup_inputs(seed: int = 0) -> dict:
    keys = jax.random.split(jax.random.key(seed), 4)
    strain = draw_strain(jax.random.fold_in(keys[3], 71), 0)
    channel_ok = place_ends((jax.random.randint(keys[1], (CHANNELS,), 0, 8) < 7).astype(jnp.int32), jax.random.fold_in(keys[1], 1), 0, 1)
    window_ok = place_ends((jax.random.randint(keys[2], (CHANNELS, WINDOWS), 0, 4) < 3).astype(jnp.int32), jax.random.fold_in(keys[2], 1), 0, 1)
    return dict(strain=strain, channel_ok=channel_ok, window_ok=window_ok)


def dft_table(first_bin, bin_count):
    bin_freq = first_bin + 1 + jnp.arange(bin_count, dtype=jnp.int32)
    sample_ids = jnp.arange(SAMPLES, dtype=jnp.int32)
    phase = (bin_freq[:, None] * sample_ids[None, :] % SAMPLES).astype(jnp.float32) * (2.0 * math.pi / SAMPLES)
    norm_scale = 1.0 / math.sqrt(SAMPLES)
    return jnp.stack([jnp.cos(phase) * norm_scale, -jnp.sin(phase) * norm_scale], axis=1).astype(jnp.bfloat16)

def reference(strain, channel_ok, window_ok):
    magnitude = jnp.abs(strain.astype(jnp.float32))
    padded = jnp.pad(magnitude, ((0, 0), (0, 0), (TIME_HALF + 1, TIME_HALF)))
    running = jnp.cumsum(padded, axis=2)
    window_sums = running[:, :, 2 * TIME_HALF + 1:] - running[:, :, :SAMPLES]
    level_mean = window_sums / (2 * TIME_HALF + 1)
    leveled = (strain.astype(jnp.float32) / (level_mean + 1e-06)).astype(jnp.bfloat16)
    table_mat = jnp.transpose(dft_table(0, BINS).astype(jnp.float32), (2, 0, 1)).reshape(SAMPLES, 2 * BINS)
    spectra = jnp.dot(leveled.astype(jnp.float32).reshape(CHANNELS * WINDOWS, SAMPLES), table_mat, precision=lax.Precision.HIGHEST, preferred_element_type=jnp.float32)
    spectra = spectra.reshape(CHANNELS, WINDOWS, BINS, 2)
    band_power = spectra[..., 0] * spectra[..., 0] + spectra[..., 1] * spectra[..., 1]
    bin_ids = jnp.arange(BINS, dtype=jnp.int32)
    smoother_ones = (jnp.abs(bin_ids[:, None] - bin_ids[None, :]) <= BIN_HALF).astype(jnp.float32)
    smooth = jnp.dot(band_power.reshape(CHANNELS * WINDOWS, BINS), smoother_ones, precision=lax.Precision.HIGHEST, preferred_element_type=jnp.float32)
    smooth = smooth.reshape(CHANNELS, WINDOWS, BINS) / (2 * BIN_HALF + 1)
    usable = (channel_ok[:, None] * window_ok).astype(jnp.float32)
    white = (spectra * (1.0 / jnp.sqrt(smooth + 1e-06))[..., None] * usable[:, :, None, None]).astype(jnp.bfloat16)
    real_in = jnp.transpose(white[..., 0], (2, 0, 1)).astype(jnp.float32)
    imag_in = jnp.transpose(white[..., 1], (2, 0, 1)).astype(jnp.float32)
    chan_ids = jnp.arange(CHANNELS, dtype=jnp.int32)
    lag_ids = jnp.arange(REACH, dtype=jnp.int32)
    partner_ids = (chan_ids[:, None] + lag_ids[None, :] + 1).astype(jnp.int32)
    back_rows = (chan_ids[:, None] + REACH - 1 - lag_ids[None, :]).astype(jnp.int32)
    back_cols = jnp.broadcast_to(lag_ids[None, :], (CHANNELS, REACH)).astype(jnp.int32)
    usable_pad = jnp.pad(usable, ((0, REACH), (0, 0)))[partner_ids]
    pair_count = lax.optimization_barrier(jnp.sum(usable[:, None, :] * usable_pad, axis=-1))
    divisor = jnp.maximum(pair_count, 1.0)

    def per_bin(inputs):
        real_row, imag_row = inputs
        real_far = jnp.pad(real_row, ((0, REACH), (0, 0)))[partner_ids]
        imag_far = jnp.pad(imag_row, ((0, REACH), (0, 0)))[partner_ids]
        real_sum = lax.optimization_barrier(jnp.sum(real_row[:, None, :] * real_far + imag_row[:, None, :] * imag_far, axis=-1))
        imag_sum = lax.optimization_barrier(jnp.sum(real_row[:, None, :] * imag_far - imag_row[:, None, :] * real_far, axis=-1))
        ahead_re = (real_sum / divisor).astype(jnp.bfloat16)
        ahead_im = (imag_sum / divisor).astype(jnp.bfloat16)
        behind_re = jnp.pad(ahead_re, ((REACH, 0), (0, 0)))[back_rows, back_cols]
        behind_im = -jnp.pad(ahead_im, ((REACH, 0), (0, 0)))[back_rows, back_cols]
        return (jnp.stack([ahead_re, ahead_im]), jnp.stack([behind_re, behind_im]))
    ahead_all, behind_all = lax.map(per_bin, (real_in, imag_in))
    return (jnp.transpose(ahead_all, (1, 0, 2, 3)), jnp.transpose(behind_all, (1, 0, 2, 3)))
```

```python
import functools
import math

import jax
import jax.numpy as jnp
from jax import lax
from jax.experimental import pallas as pl
from jax.experimental.pallas import tpu as pltpu
from jax.sharding import PartitionSpec as P

WINDOWS = 8
SAMPLES = 2048
REACH = 128
TIME_HALF = 128
BIN_HALF = 32
LOCAL = 32
AHEAD = REACH // LOCAL
BLOCK = 256
ROWS = LOCAL * WINDOWS
GROUPS = 2
CHUNKS = 2
STEPS = 4
F32 = jnp.float32
BF16 = jnp.bfloat16
MESH = pl.DeviceIdType.MESH

SLOT_AHEAD = (0, 1, 2, 3, 8)
SLOT_BEHIND = (5, 6, 7, 4, 9)
SLOTS = 12


def iota(shape, axis):
    return lax.broadcasted_iota(jnp.int32, shape, axis)


def cos_sin(index):
    quarter = SAMPLES // 4
    turn = (index + quarter // 2) // quarter
    x = (index - turn * quarter).astype(F32) * (2.0 * math.pi / SAMPLES)
    y = x * x
    s = x * (1.0 + y * (-1 / 6 + y * (1 / 120 + y * (-1 / 5040 + y * (1 / 362880)))))
    c = 1.0 + y * (-1 / 2 + y * (1 / 24 + y * (-1 / 720 + y * (1 / 40320))))
    turn = turn & 3
    odd = (turn & 1) == 1
    cos = jnp.where(odd, s, c)
    sin = jnp.where(odd, c, s)
    cos = jnp.where((turn == 1) | (turn == 2), -cos, cos)
    sin = jnp.where(turn >= 2, -sin, sin)
    return cos, sin


def lane_bin(lane):
    block = lane // 64
    within = (lane // 32) % 2 * 16 + lane % 16
    return within + jnp.where(block == 1, -LOCAL, jnp.where(block == 2, LOCAL, 0))


def front_kernel(
    ahead_count, bins, strain_ref, ok_ref, window_ref, gath_ref, use_ref,
    x_ref, table_ref, base_ref, ring_ref, spread_ref, band_ref, white_ref,
    in_sem, use_send, use_recv, send_sem, recv_sem,
):
    me = lax.axis_index("ch")
    first_bin = lax.axis_index("freq") * LOCAL + 1
    rows = ROWS // CHUNKS
    channels = LOCAL // CHUNKS

    loads = []
    for chunk in range(CHUNKS):
        part = pl.ds(chunk * rows, rows)
        loads.append(pltpu.make_async_copy(strain_ref.at[part], x_ref.at[part], in_sem.at[chunk]))
        loads[-1].start()

    barrier = pltpu.get_barrier_semaphore()
    peers = jnp.int32(0)
    for distance in range(1, AHEAD + 1):
        for step in (distance, -distance):
            there = (me + step >= 0) & (me + step < ahead_count)
            peers = peers + there.astype(jnp.int32)

            @pl.when(there)
            def _():
                pl.semaphore_signal(barrier, 1, device_id={"ch": me + step}, device_id_type=MESH)

    diagonal = iota((LOCAL, LOCAL), 0) == iota((LOCAL, LOCAL), 1)
    healthy = jnp.sum(jnp.where(diagonal, ok_ref[...].astype(F32), 0.0), axis=1, keepdims=True)
    usable8 = (window_ref[...].astype(F32) * healthy).astype(BF16)
    widen = (iota((WINDOWS, 128), 0) == iota((WINDOWS, 128), 1)).astype(BF16)
    usable = jnp.dot(usable8, widen, preferred_element_type=F32).astype(BF16)
    flip = (iota((LOCAL, LOCAL), 0) + iota((LOCAL, LOCAL), 1) == LOCAL - 1).astype(BF16)
    use_ref[SLOT_AHEAD[0]] = usable
    use_ref[SLOT_BEHIND[0]] = jnp.dot(flip, usable, preferred_element_type=F32).astype(BF16)
    keep = []
    for half in range(2):
        expand = (iota((128, 128), 0) == 4 * half + iota((128, 128), 1) // 32).astype(BF16)
        keep.append(jnp.dot(usable, expand, preferred_element_type=F32))

    for slot in range(10, SLOTS):
        gath_ref[slot] = jnp.zeros((LOCAL, 512), BF16)
        use_ref[slot] = jnp.zeros((LOCAL, 128), BF16)
    for distance in range(1, AHEAD + 1):
        for step, slot in ((distance, SLOT_AHEAD[distance]), (-distance, SLOT_BEHIND[distance])):
            absent = (me + step < 0) | (me + step >= ahead_count)

            @pl.when(absent)
            def _():
                gath_ref[slot] = jnp.zeros((LOCAL, 512), BF16)
                use_ref[slot] = jnp.zeros((LOCAL, 128), BF16)

    distance_in = iota((2 * BLOCK, BLOCK), 0) - TIME_HALF - iota((2 * BLOCK, BLOCK), 1)
    spread_ref[...] = (jnp.abs(distance_in) <= TIME_HALF).astype(BF16)

    source = iota((BLOCK, 128), 0)
    target = iota((BLOCK, 128), 1)
    source_bin = lane_bin(source) + first_bin
    near = jnp.abs(source_bin - (lane_bin(target) + first_bin)) <= BIN_HALF
    inside = (source_bin >= 1) & (source_bin <= bins) & (source < 192) & (target < 64)
    band_ref[...] = (near & inside).astype(BF16)

    row = iota((48, BLOCK), 0)
    step_of = jnp.where(row < 32, 8 * row, jnp.where(row < 40, row - 32, 256 * (row - 40)))
    lane = iota((48, BLOCK), 1)
    cos, sin = cos_sin(((lane_bin(lane) + first_bin) * step_of) & (SAMPLES - 1))
    imaginary = (iota((8, BLOCK), 1) // 16) % 2 == 1
    cos1, sin1 = cos[32:40], sin[32:40]
    for i in range(32):
        c8, s8 = cos[i : i + 1], sin[i : i + 1]
        c = c8 * cos1 - s8 * sin1
        s = s8 * cos1 + c8 * sin1
        base_ref[0, pl.ds(8 * i, 8)] = jnp.where(imaginary, -s, c)
        base_ref[1, pl.ds(8 * i, 8)] = jnp.where(imaginary, -c, -s)
    scale = 1.0 / math.sqrt(SAMPLES)
    ring_ref[0] = cos[40:48] * scale
    ring_ref[1] = sin[40:48] * scale
    for c in range(SAMPLES // BLOCK):
        table_ref[pl.ds(c * BLOCK, BLOCK)] = (
            base_ref[0] * ring_ref[0, pl.ds(c, 1)] + base_ref[1] * ring_ref[1, pl.ds(c, 1)]
        ).astype(BF16)

    pl.semaphore_wait(barrier, peers)

    def copies(step, part):
        own, slot = (SLOT_BEHIND[0], SLOT_BEHIND[step]) if step > 0 else (SLOT_AHEAD[0], SLOT_AHEAD[-step])
        which = (step + AHEAD) if step < 0 else (step + AHEAD - 1)
        if part is None:
            src, dst, send, recv = use_ref.at[own], use_ref.at[slot], use_send.at[which], use_recv.at[which]
        else:
            at = pl.ds((CHUNKS - 1 - part if step > 0 else part) * channels, channels)
            src, dst = gath_ref.at[own, at], gath_ref.at[slot, at]
            send, recv = send_sem.at[part, which], recv_sem.at[part, which]
        return pltpu.make_async_remote_copy(
            src_ref=src, dst_ref=dst, send_sem=send, recv_sem=recv, device_id={"ch": me + step}, device_id_type=MESH
        )

    steps = [s * d for d in range(AHEAD, 0, -1) for s in (1, -1)]

    def for_each(part, act):
        for step in steps:
            @pl.when((me + step >= 0) & (me + step < ahead_count))
            def _():
                act(copies(step, part))

    def for_each_source(part, act):
        for step in steps:
            @pl.when((me - step >= 0) & (me - step < ahead_count))
            def _():
                act(copies(step, part))

    for_each(None, lambda copy: copy.start())

    lanes = iota((channels, 128), 1) // 32
    flip = (iota((channels, channels), 0) + iota((channels, channels), 1) == channels - 1).astype(BF16)
    for chunk in range(CHUNKS):
        loads[chunk].wait()
        part = pl.ds(chunk * rows, rows)
        spectrum = jnp.zeros((rows, BLOCK), F32)
        for block in range(SAMPLES // BLOCK):
            low = max(block * BLOCK - TIME_HALF, 0)
            high = min(block * BLOCK + BLOCK + TIME_HALF, SAMPLES)
            skip = low - (block * BLOCK - TIME_HALF)
            sums = jnp.dot(
                jnp.abs(x_ref[part, low:high]), spread_ref[skip : skip + high - low], preferred_element_type=F32
            )
            level = sums * (1.0 / (2 * TIME_HALF + 1)) + 1e-06
            leveled = (x_ref[part, block * BLOCK : (block + 1) * BLOCK].astype(F32) / level).astype(BF16)
            spectrum = spectrum + jnp.dot(
                leveled, table_ref[block * BLOCK : (block + 1) * BLOCK], preferred_element_type=F32
            )
        power = spectrum * spectrum
        coarse = power.astype(BF16)
        fine = (power - coarse.astype(F32)).astype(BF16)
        smooth = jnp.dot(coarse, band_ref[...], preferred_element_type=F32) + jnp.dot(
            fine, band_ref[...], preferred_element_type=F32
        )
        white_ref[part] = spectrum[:, :128] * lax.rsqrt(smooth * (1.0 / (2 * BIN_HALF + 1)) + 1e-06)
        at = chunk * channels
        by_window = [white_ref[pl.ds(chunk * rows + w, channels, stride=WINDOWS)] for w in range(WINDOWS)]
        for group in range(GROUPS):
            for half in range(2):
                piece = None
                for i in range(4):
                    moved = pltpu.roll(by_window[4 * half + i], (32 * (i - group)) % 128, 1)
                    piece = moved if piece is None else jnp.where(lanes == i, moved, piece)
                piece = (piece * keep[half][at : at + channels]).astype(BF16)
                where = pl.ds((2 * group + half) * 128, 128)
                gath_ref[SLOT_AHEAD[0], pl.ds(at, channels), where] = piece
                gath_ref[SLOT_BEHIND[0], pl.ds(LOCAL - at - channels, channels), where] = jnp.dot(
                    flip, piece, preferred_element_type=F32
                ).astype(BF16)
        for_each(chunk, lambda copy: copy.start())

    for part in (None, *range(CHUNKS)):
        for_each_source(part, lambda copy: copy.wait_recv())
        for_each(part, lambda copy: copy.wait_send())


def front(strain, channel_ok, window_ok, ahead_count, bins):
    return pl.pallas_call(
        functools.partial(front_kernel, ahead_count, bins),
        out_shape=(
            jax.ShapeDtypeStruct((SLOTS, LOCAL, 512), BF16),
            jax.ShapeDtypeStruct((SLOTS, LOCAL, 128), BF16),
        ),
        in_specs=[
            pl.BlockSpec(memory_space=pl.ANY),
            pl.BlockSpec(memory_space=pltpu.VMEM),
            pl.BlockSpec(memory_space=pltpu.VMEM),
        ],
        out_specs=(pl.BlockSpec(memory_space=pltpu.VMEM), pl.BlockSpec(memory_space=pltpu.VMEM)),
        scratch_shapes=[
            pltpu.VMEM((ROWS, SAMPLES), BF16),
            pltpu.VMEM((SAMPLES, BLOCK), BF16),
            pltpu.VMEM((2, BLOCK, BLOCK), F32),
            pltpu.VMEM((2, 8, BLOCK), F32),
            pltpu.VMEM((2 * BLOCK, BLOCK), BF16),
            pltpu.VMEM((BLOCK, 128), BF16),
            pltpu.VMEM((ROWS, 128), F32),
            pltpu.SemaphoreType.DMA((CHUNKS,)),
            pltpu.SemaphoreType.DMA((2 * AHEAD,)),
            pltpu.SemaphoreType.DMA((2 * AHEAD,)),
            pltpu.SemaphoreType.DMA((CHUNKS, 2 * AHEAD)),
            pltpu.SemaphoreType.DMA((CHUNKS, 2 * AHEAD)),
        ],
        compiler_params=pltpu.CompilerParams(collective_id=0, has_side_effects=True),
        name="front",
    )(strain.reshape(ROWS, SAMPLES), channel_ok.reshape(1, LOCAL), window_ok)


def lag_rows(ahead, behind, tail):
    row = iota((LOCAL, 128), 0)
    lane = iota((LOCAL, 128), 1)
    ahead = jnp.where(lane <= row, tail, ahead)
    behind = jnp.where((lane >= 32) & (lane < 64 - row), tail, behind)
    return (
        jnp.take_along_axis(ahead, (lane + row + 1) & 127, axis=1),
        pltpu.roll(behind, 64, 1, stride=1, stride_axis=0),
    )


def cross_kernel(gath_ref, use_ref, ahead_ref, behind_ref, scale_ref, lhs_ref):
    step = pl.program_id(0)
    per_step = LOCAL // STEPS

    @pl.when(step == 0)
    def _():
        pairs = lax.dot_general(
            use_ref[0], use_ref[...].reshape(SLOTS * LOCAL, 128), (((1,), (1,)), ((), ())), preferred_element_type=F32
        )
        for side, count in enumerate(lag_rows(pairs[:, :128], pairs[:, 128:256], pairs[:, 256:])):
            scale_ref[side] = 1.0 / jnp.maximum(count, 1.0)

    at = pl.ds(pl.multiple_of(step // (STEPS // GROUPS) * 256, 256), 256)
    own = gath_ref[0, :, at]
    wide = own.astype(F32)
    swap = jnp.where((iota((LOCAL, 256), 1) // 16) % 2 == 0, -pltpu.roll(wide, 240, 1), pltpu.roll(wide, 16, 1)).astype(BF16)
    lane_of = iota((LOCAL, 256), 1) % 16
    first = step % (STEPS // GROUPS) * per_step
    for part, value in enumerate((own, swap)):
        for f in range(per_step):
            lhs_ref[pl.ds((part * per_step + f) * LOCAL, LOCAL)] = jnp.where(
                lane_of == first + f, value, jnp.zeros_like(value)
            )
    rhs = gath_ref[:, :, at].reshape(SLOTS * LOCAL, 256)
    cross = lax.dot_general(lhs_ref[...], rhs, (((1,), (1,)), ((), ())), preferred_element_type=F32)
    for part in range(2):
        for f in range(per_step):
            rows = slice((part * per_step + f) * LOCAL, (part * per_step + f + 1) * LOCAL)
            ahead, behind = lag_rows(cross[rows, :128], cross[rows, 128:256], cross[rows, 256:])
            ahead_ref[part, f] = (ahead * scale_ref[0]).astype(BF16)
            behind_ref[part, f] = (behind * scale_ref[1]).astype(BF16)


def cross(gathered, usable):
    per_step = LOCAL // STEPS
    out = jax.ShapeDtypeStruct((2, LOCAL, LOCAL, REACH), BF16)
    out_spec = pl.BlockSpec((2, per_step, LOCAL, REACH), lambda i: (0, i, 0, 0))
    return pl.pallas_call(
        cross_kernel,
        grid=(STEPS,),
        out_shape=(out, out),
        in_specs=[pl.BlockSpec(memory_space=pltpu.VMEM), pl.BlockSpec(memory_space=pltpu.VMEM)],
        out_specs=(out_spec, out_spec),
        scratch_shapes=[
            pltpu.VMEM((2, LOCAL, 128), F32),
            pltpu.VMEM((2 * per_step * LOCAL, 256), BF16),
        ],
        name="cross",
    )(gathered, usable)


def solution(mesh):
    ahead_count = mesh.shape["ch"]
    bins = LOCAL * mesh.shape["freq"]

    def per_device(strain, channel_ok, window_ok):
        gathered, usable = front(strain, channel_ok, window_ok, ahead_count, bins)
        return cross(gathered, usable)

    return jax.shard_map(
        per_device,
        mesh=mesh,
        in_specs=(P("ch", None, None), P("ch"), P("ch", None)),
        out_specs=(P(None, "freq", "ch", None), P(None, "freq", "ch", None)),
        check_vma=False,
    )
```

```python
import functools
import math

import jax
import jax.numpy as jnp
from jax import lax
from jax.experimental import pallas as pl
from jax.experimental.pallas import tpu as pltpu
from jax.sharding import PartitionSpec as P

WINDOWS = 8
SAMPLES = 2048
REACH = 128
TIME_HALF = 128
BIN_HALF = 32
LOCAL = 32
AHEAD = REACH // LOCAL
BLOCK = 256
ROWS = LOCAL * WINDOWS
GROUPS = 2
CHUNKS = 1
VMEM_LIMIT = 24 << 20
STEPS = 4
F32 = jnp.float32
BF16 = jnp.bfloat16
MESH = pl.DeviceIdType.MESH

SLOT_AHEAD = (0, 1, 2, 3, 8)
SLOT_BEHIND = (5, 6, 7, 4, 9)
SLOTS = 12


def iota(shape, axis):
    return lax.broadcasted_iota(jnp.int32, shape, axis)


def cos_sin(index):
    quarter = SAMPLES // 4
    turn = (index + quarter // 2) // quarter
    x = (index - turn * quarter).astype(F32) * (2.0 * math.pi / SAMPLES)
    y = x * x
    s = x * (1.0 + y * (-1 / 6 + y * (1 / 120 + y * (-1 / 5040 + y * (1 / 362880)))))
    c = 1.0 + y * (-1 / 2 + y * (1 / 24 + y * (-1 / 720 + y * (1 / 40320))))
    turn = turn & 3
    odd = (turn & 1) == 1
    cos = jnp.where(odd, s, c)
    sin = jnp.where(odd, c, s)
    cos = jnp.where((turn == 1) | (turn == 2), -cos, cos)
    sin = jnp.where(turn >= 2, -sin, sin)
    return cos, sin


def lane_bin(lane):
    block = lane // 64
    within = (lane // 32) % 2 * 16 + lane % 16
    return within + jnp.where(block == 1, -LOCAL, jnp.where(block == 2, LOCAL, 0))


def write_spread(spread_ref):
    half = BLOCK // 2
    row, lane = iota((half, half), 0), iota((half, half), 1)
    lower = (row >= lane).astype(BF16)
    upper = (row <= lane).astype(BF16)
    ones = jnp.ones((half, half), BF16)
    zeros = jnp.zeros((half, half), BF16)
    for i, pair in enumerate(((lower, zeros), (ones, lower), (upper, ones), (zeros, upper))):
        for j, piece in enumerate(pair):
            spread_ref[i * half : (i + 1) * half, j * half : (j + 1) * half] = piece


def write_band(band_ref, below, above):
    shape = (16, 128)
    target = iota(shape, 1) // 32 % 2 * 16 + iota(shape, 1) % 16
    for group in range(GROUPS):
        source = iota(shape, 0) + 16 * group
        pieces = (
            jnp.ones(shape, BF16),
            jnp.where(source >= target, below, 0.0).astype(BF16),
            jnp.where(source <= target, above, 0.0).astype(BF16),
            jnp.zeros(shape, BF16),
        )
        for block, piece in enumerate(pieces):
            for part in range(2):
                band_ref[pl.ds(block * 64 + group * 32 + part * 16, 16)] = piece


def write_table(table_ref, angle_ref, first_bin):
    row = iota((48, BLOCK), 0)
    step_of = jnp.where(row < 32, 8 * row, jnp.where(row < 40, row - 32, 256 * (row - 40)))
    bin_of = lane_bin(iota((48, BLOCK), 1)) + first_bin
    cos, sin = cos_sin((bin_of * step_of) & (SAMPLES - 1))
    scale = 1.0 / math.sqrt(SAMPLES)
    angle_ref[0] = cos[:40] * scale
    angle_ref[1] = sin[:40] * scale
    imaginary = (iota((8, BLOCK), 1) // 16) % 2 == 1
    cos1, sin1 = cos[32:40], sin[32:40]
    same_c, same_s = jnp.where(imaginary, -sin1, cos1), jnp.where(imaginary, -cos1, -sin1)
    next_c, next_s = same_s, -same_c
    cos8 = jnp.broadcast_to(cos[41:42], (16, BLOCK))
    sin8 = jnp.broadcast_to(sin[41:42], (16, BLOCK))
    quarter = (lane_bin(iota((16, BLOCK), 1)) + first_bin) & 3
    real4 = jnp.where(quarter == 0, 1.0, jnp.where(quarter == 2, -1.0, 0.0)).astype(BF16)
    imag4 = jnp.where(quarter == 1, 1.0, jnp.where(quarter == 3, -1.0, 0.0)).astype(BF16)
    sign2 = jnp.where((quarter & 1) == 0, 1.0, -1.0).astype(BF16)
    for t in range(BLOCK // 16):
        x, y = [], []
        for i in (2 * t, 2 * t + 1):
            c = jnp.broadcast_to(angle_ref[0, pl.ds(i, 1)], (8, BLOCK))
            s = jnp.broadcast_to(angle_ref[1, pl.ds(i, 1)], (8, BLOCK))
            x.append(c * same_c + s * same_s)
            y.append(c * next_c + s * next_s)
        x, y = jnp.concatenate(x, axis=0), jnp.concatenate(y, axis=0)
        for c, (u, v) in enumerate(((x, y), (x * cos8 + y * sin8, y * cos8 - x * sin8))):
            u, v = u.astype(BF16), v.astype(BF16)
            turned = u * real4 + v * imag4
            for step, value in ((c, u), (c + 2, turned), (c + 4, u * sign2), (c + 6, turned * sign2)):
                table_ref[pl.ds(step * BLOCK + 16 * t, 16)] = value


def front_kernel(
    ahead_count, freq_count, strain_ref, ok_hbm, window_hbm, gath_ref, use_ref,
    x_ref, ok_ref, window_ref, table_ref, angle_ref, spread_ref, band_ref, white_ref,
    in_sem, small_sem, use_send, use_recv, send_sem, recv_sem,
):
    me = lax.axis_index("ch")
    freq = lax.axis_index("freq")
    first_bin = freq * LOCAL + 1
    rows = ROWS // CHUNKS
    channels = LOCAL // CHUNKS

    small = [
        pltpu.make_async_copy(ok_hbm, ok_ref, small_sem.at[0]),
        pltpu.make_async_copy(window_hbm, window_ref, small_sem.at[1]),
    ]
    for load in small:
        load.start()
    loads = []
    for chunk in range(CHUNKS):
        part = pl.ds(chunk * rows, rows)
        loads.append(pltpu.make_async_copy(strain_ref.at[part], x_ref.at[part], in_sem.at[chunk]))
        loads[-1].start()

    barrier = pltpu.get_barrier_semaphore()
    peers = jnp.int32(0)
    for distance in range(1, AHEAD + 1):
        for step in (distance, -distance):
            there = (me + step >= 0) & (me + step < ahead_count)
            peers = peers + there.astype(jnp.int32)

            @pl.when(there)
            def _():
                pl.semaphore_signal(barrier, 1, device_id={"ch": me + step}, device_id_type=MESH)

    write_table(table_ref, angle_ref, first_bin)
    write_spread(spread_ref)
    write_band(band_ref, (freq > 0).astype(F32), (freq < freq_count - 1).astype(F32))

    for slot in range(10, SLOTS):
        gath_ref[slot] = jnp.zeros((LOCAL, 512), BF16)
        use_ref[slot] = jnp.zeros((LOCAL, 128), BF16)

    @pl.when((me < AHEAD) | (me >= ahead_count - AHEAD))
    def _():
        for distance in range(1, AHEAD + 1):
            for step, slot in ((distance, SLOT_AHEAD[distance]), (-distance, SLOT_BEHIND[distance])):

                @pl.when((me + step < 0) | (me + step >= ahead_count))
                def _():
                    gath_ref[slot] = jnp.zeros((LOCAL, 512), BF16)
                    use_ref[slot] = jnp.zeros((LOCAL, 128), BF16)

    for load in small:
        load.wait()
    usable8 = (window_ref[...].astype(F32) * ok_ref[...].astype(F32)).astype(BF16)
    widen = (iota((WINDOWS, 128), 0) == iota((WINDOWS, 128), 1)).astype(BF16)
    usable = lax.dot_general(usable8, widen, (((0,), (0,)), ((), ())), preferred_element_type=F32).astype(BF16)
    flip = (iota((LOCAL, LOCAL), 0) + iota((LOCAL, LOCAL), 1) == LOCAL - 1).astype(BF16)
    use_ref[SLOT_AHEAD[0]] = usable
    use_ref[SLOT_BEHIND[0]] = jnp.dot(flip, usable, preferred_element_type=F32).astype(BF16)
    keep = []
    for half in range(2):
        expand = (iota((128, 128), 0) == 4 * half + iota((128, 128), 1) // 32).astype(BF16)
        keep.append(jnp.dot(usable, expand, preferred_element_type=F32))

    pl.semaphore_wait(barrier, peers)

    def copies(step, part):
        own, slot = (SLOT_BEHIND[0], SLOT_BEHIND[step]) if step > 0 else (SLOT_AHEAD[0], SLOT_AHEAD[-step])
        which = (step + AHEAD) if step < 0 else (step + AHEAD - 1)
        if part is None:
            src, dst, send, recv = use_ref.at[own], use_ref.at[slot], use_send.at[which], use_recv.at[which]
        else:
            at = pl.ds((CHUNKS - 1 - part if step > 0 else part) * channels, channels)
            src, dst = gath_ref.at[own, at], gath_ref.at[slot, at]
            send, recv = send_sem.at[part, which], recv_sem.at[part, which]
        return pltpu.make_async_remote_copy(
            src_ref=src, dst_ref=dst, send_sem=send, recv_sem=recv, device_id={"ch": me + step}, device_id_type=MESH
        )

    steps = [s * d for d in range(AHEAD, 0, -1) for s in (1, -1)]

    def for_each(part, act):
        for step in steps:
            @pl.when((me + step >= 0) & (me + step < ahead_count))
            def _():
                act(copies(step, part))

    def for_each_source(part, act):
        for step in steps:
            @pl.when((me - step >= 0) & (me - step < ahead_count))
            def _():
                act(copies(step, part))

    for_each(None, lambda copy: copy.start())

    lanes = iota((channels, 128), 1) // 32
    flip = (iota((channels, channels), 0) + iota((channels, channels), 1) == channels - 1).astype(BF16)
    for chunk in range(CHUNKS):
        loads[chunk].wait()
        part = pl.ds(chunk * rows, rows)
        spectrum = jnp.zeros((rows, BLOCK), F32)
        for block in range(SAMPLES // BLOCK):
            low = max(block * BLOCK - TIME_HALF, 0)
            high = min(block * BLOCK + BLOCK + TIME_HALF, SAMPLES)
            skip = low - (block * BLOCK - TIME_HALF)
            sums = jnp.dot(
                jnp.abs(x_ref[part, low:high]), spread_ref[skip : skip + high - low], preferred_element_type=F32
            )
            level = sums * (1.0 / (2 * TIME_HALF + 1)) + 1e-06
            leveled = (x_ref[part, block * BLOCK : (block + 1) * BLOCK].astype(F32) / level).astype(BF16)
            spectrum = spectrum + jnp.dot(
                leveled, table_ref[block * BLOCK : (block + 1) * BLOCK], preferred_element_type=F32
            )
        power = spectrum * spectrum
        coarse = power.astype(BF16)
        fine = (power - coarse.astype(F32)).astype(BF16)
        smooth = jnp.dot(coarse, band_ref[...], preferred_element_type=F32) + jnp.dot(
            fine, band_ref[...], preferred_element_type=F32
        )
        white_ref[part] = spectrum[:, :128] * lax.rsqrt(smooth * (1.0 / (2 * BIN_HALF + 1)) + 1e-06)
        at = chunk * channels
        by_window = [white_ref[pl.ds(chunk * rows + w, channels, stride=WINDOWS)] for w in range(WINDOWS)]
        for group in range(GROUPS):
            for half in range(2):
                piece = None
                for i in range(4):
                    moved = pltpu.roll(by_window[4 * half + i], (32 * (i - group)) % 128, 1)
                    piece = moved if piece is None else jnp.where(lanes == i, moved, piece)
                piece = (piece * keep[half][at : at + channels]).astype(BF16)
                where = pl.ds((2 * group + half) * 128, 128)
                gath_ref[SLOT_AHEAD[0], pl.ds(at, channels), where] = piece
                gath_ref[SLOT_BEHIND[0], pl.ds(LOCAL - at - channels, channels), where] = jnp.dot(
                    flip, piece, preferred_element_type=F32
                ).astype(BF16)
        for_each(chunk, lambda copy: copy.start())

    for part in (None, *range(CHUNKS)):
        for_each_source(part, lambda copy: copy.wait_recv())
        for_each(part, lambda copy: copy.wait_send())


def front(strain, channel_ok, window_ok, ahead_count, freq_count):
    hbm = pl.BlockSpec(memory_space=pltpu.MemorySpace.HBM)
    vmem = pl.BlockSpec(memory_space=pltpu.VMEM)
    args = (strain.reshape(ROWS, SAMPLES), channel_ok.reshape(1, LOCAL), window_ok.T)
    return pl.pallas_call(
        functools.partial(front_kernel, ahead_count, freq_count),
        out_shape=(
            jax.ShapeDtypeStruct((SLOTS, LOCAL, 512), BF16),
            jax.ShapeDtypeStruct((SLOTS, LOCAL, 128), BF16),
        ),
        in_specs=[hbm, hbm, hbm],
        out_specs=(vmem, vmem),
        scratch_shapes=[
            pltpu.VMEM((ROWS, SAMPLES), BF16),
            pltpu.VMEM((1, LOCAL), jnp.int32),
            pltpu.VMEM((WINDOWS, LOCAL), jnp.int32),
            pltpu.VMEM((SAMPLES, BLOCK), BF16),
            pltpu.VMEM((2, 40, BLOCK), F32),
            pltpu.VMEM((2 * BLOCK, BLOCK), BF16),
            pltpu.VMEM((BLOCK, 128), BF16),
            pltpu.VMEM((ROWS, 128), F32),
            pltpu.SemaphoreType.DMA((CHUNKS,)),
            pltpu.SemaphoreType.DMA((2,)),
            pltpu.SemaphoreType.DMA((2 * AHEAD,)),
            pltpu.SemaphoreType.DMA((2 * AHEAD,)),
            pltpu.SemaphoreType.DMA((CHUNKS, 2 * AHEAD)),
            pltpu.SemaphoreType.DMA((CHUNKS, 2 * AHEAD)),
        ],
        compiler_params=pltpu.CompilerParams(collective_id=0, has_side_effects=True, vmem_limit_bytes=VMEM_LIMIT),
        name="front",
    )(*(pltpu.with_memory_space_constraint(arg, pltpu.HBM) for arg in args))


def lag_rows(ahead, behind, tail):
    row = iota((LOCAL, 128), 0)
    lane = iota((LOCAL, 128), 1)
    ahead = jnp.where(lane <= row, tail, ahead)
    behind = jnp.where((lane >= 32) & (lane < 64 - row), tail, behind)
    return (
        jnp.take_along_axis(ahead, (lane + row + 1) & 127, axis=1),
        pltpu.roll(behind, 64, 1, stride=1, stride_axis=0),
    )


def cross_kernel(gath_ref, use_ref, ahead_hbm, behind_hbm, ahead_ref, behind_ref, out_sem):
    contract = (((1,), (1,)), ((), ()))
    per_step = LOCAL // STEPS
    pairs = lax.dot_general(use_ref[0], use_ref[...].reshape(SLOTS * LOCAL, 128), contract, preferred_element_type=F32)
    scales = [1.0 / jnp.maximum(n, 1.0) for n in lag_rows(pairs[:, :128], pairs[:, 128:256], pairs[:, 256:])]
    lane_of = iota((LOCAL, 256), 1) % 16
    imaginary = (iota((LOCAL, 256), 1) // 16) % 2 == 1
    copies = []
    for step in range(STEPS):
        group, first = divmod(step * per_step, 16)
        at = slice(group * 256, (group + 1) * 256)
        own = gath_ref[0, :, at]
        wide = own.astype(F32)
        swap = jnp.where(imaginary, pltpu.roll(wide, 16, 1), -pltpu.roll(wide, 240, 1)).astype(BF16)
        lhs = jnp.concatenate(
            [
                jnp.where(lane_of == first + f, value, jnp.zeros_like(value))
                for value in (own, swap)
                for f in range(per_step)
            ],
            axis=0,
        )
        rhs = gath_ref[:, :, at].reshape(SLOTS * LOCAL, 256)
        cross = lax.dot_general(lhs, rhs, contract, preferred_element_type=F32)
        for part in range(2):
            for f in range(per_step):
                rows = slice((part * per_step + f) * LOCAL, (part * per_step + f + 1) * LOCAL)
                ahead, behind = lag_rows(cross[rows, :128], cross[rows, 128:256], cross[rows, 256:])
                ahead_ref[part, step * per_step + f] = (ahead * scales[0]).astype(BF16)
                behind_ref[part, step * per_step + f] = (behind * scales[1]).astype(BF16)
        done = pl.ds(step * per_step, per_step)
        for side, (src, dst) in enumerate(((ahead_ref, ahead_hbm), (behind_ref, behind_hbm))):
            copies.append(pltpu.make_async_copy(src.at[:, done], dst.at[:, done], out_sem.at[side, step]))
            copies[-1].start()
    for copy in copies:
        copy.wait()


def cross(gathered, usable):
    shape = (2, LOCAL, LOCAL, REACH)
    vmem = pl.BlockSpec(memory_space=pltpu.VMEM)
    hbm = pl.BlockSpec(memory_space=pltpu.MemorySpace.HBM)
    return pl.pallas_call(
        cross_kernel,
        out_shape=(jax.ShapeDtypeStruct(shape, BF16), jax.ShapeDtypeStruct(shape, BF16)),
        in_specs=[vmem, vmem],
        out_specs=(hbm, hbm),
        scratch_shapes=[pltpu.VMEM(shape, BF16), pltpu.VMEM(shape, BF16), pltpu.SemaphoreType.DMA((2, STEPS))],
        compiler_params=pltpu.CompilerParams(vmem_limit_bytes=VMEM_LIMIT),
        name="cross",
    )(gathered, usable)


def solution(mesh):
    ahead_count = mesh.shape["ch"]
    freq_count = mesh.shape["freq"]

    def per_device(strain, channel_ok, window_ok):
        gathered, usable = front(strain, channel_ok, window_ok, ahead_count, freq_count)
        return cross(gathered, usable)

    return jax.shard_map(
        per_device,
        mesh=mesh,
        in_specs=(P("ch", None, None), P("ch"), P("ch", None)),
        out_specs=(P(None, "freq", "ch", None), P(None, "freq", "ch", None)),
        check_vma=False,
    )
```

```python
import functools
import math

import jax
import jax.numpy as jnp
from jax import lax
from jax.experimental import pallas as pl
from jax.experimental.pallas import tpu as pltpu
from jax.sharding import PartitionSpec as P

WINDOWS = 8
SAMPLES = 2048
REACH = 128
TIME_HALF = 128
BIN_HALF = 32
LOCAL = 32
AHEAD = REACH // LOCAL
BLOCK = 256
ROWS = LOCAL * WINDOWS
GROUPS = 2
TALL = 4 * LOCAL + WINDOWS
VMEM_LIMIT = 24 << 20
STEPS = 4
F32 = jnp.float32
BF16 = jnp.bfloat16
MESH = pl.DeviceIdType.MESH

SLOT_AHEAD = (0, 1, 2, 3, 8)
SLOT_BEHIND = (5, 6, 7, 4, 9)
SLOTS = 12


def iota(shape, axis):
    return lax.broadcasted_iota(jnp.int32, shape, axis)


def cos_sin(index):
    quarter = SAMPLES // 4
    turn = (index + quarter // 2) // quarter
    x = (index - turn * quarter).astype(F32) * (2.0 * math.pi / SAMPLES)
    y = x * x
    s = x * (1.0 + y * (-1 / 6 + y * (1 / 120 + y * (-1 / 5040 + y * (1 / 362880)))))
    c = 1.0 + y * (-1 / 2 + y * (1 / 24 + y * (-1 / 720 + y * (1 / 40320))))
    turn = turn & 3
    odd = (turn & 1) == 1
    cos = jnp.where(odd, s, c)
    sin = jnp.where(odd, c, s)
    cos = jnp.where((turn == 1) | (turn == 2), -cos, cos)
    sin = jnp.where(turn >= 2, -sin, sin)
    return cos, sin


def lane_bin(lane):
    block = lane // 64
    within = (lane // 32) % 2 * 16 + lane % 16
    return within + jnp.where(block == 1, -LOCAL, jnp.where(block == 2, LOCAL, 0))


def write_spread(spread_ref):
    half = BLOCK // 2
    row, lane = iota((half, half), 0), iota((half, half), 1)
    lower = (row >= lane).astype(BF16)
    upper = (row <= lane).astype(BF16)
    ones = jnp.ones((half, half), BF16)
    zeros = jnp.zeros((half, half), BF16)
    for i, pair in enumerate(((lower, zeros), (ones, lower), (upper, ones), (zeros, upper))):
        for j, piece in enumerate(pair):
            spread_ref[i * half : (i + 1) * half, j * half : (j + 1) * half] = piece


def write_band(band_ref, below, above):
    shape = (16, 128)
    target = iota(shape, 1) // 32 % 2 * 16 + iota(shape, 1) % 16
    for group in range(GROUPS):
        source = iota(shape, 0) + 16 * group
        pieces = (
            jnp.ones(shape, BF16),
            jnp.where(source >= target, below, 0.0).astype(BF16),
            jnp.where(source <= target, above, 0.0).astype(BF16),
            jnp.zeros(shape, BF16),
        )
        for block, piece in enumerate(pieces):
            for part in range(2):
                band_ref[pl.ds(block * 64 + group * 32 + part * 16, 16)] = piece


def write_table(table_ref, angle_ref, first_bin):
    row = iota((48, BLOCK), 0)
    step_of = jnp.where(row < 32, 8 * row, jnp.where(row < 40, row - 32, 256 * (row - 40)))
    bin_of = lane_bin(iota((48, BLOCK), 1)) + first_bin
    cos, sin = cos_sin((bin_of * step_of) & (SAMPLES - 1))
    scale = 1.0 / math.sqrt(SAMPLES)
    angle_ref[0] = cos[:40] * scale
    angle_ref[1] = sin[:40] * scale
    imaginary = (iota((8, BLOCK), 1) // 16) % 2 == 1
    cos1, sin1 = cos[32:40], sin[32:40]
    same_c, same_s = jnp.where(imaginary, -sin1, cos1), jnp.where(imaginary, -cos1, -sin1)
    next_c, next_s = same_s, -same_c
    cos8 = jnp.broadcast_to(cos[41:42], (16, BLOCK))
    sin8 = jnp.broadcast_to(sin[41:42], (16, BLOCK))
    quarter = (lane_bin(iota((16, BLOCK), 1)) + first_bin) & 3
    real4 = jnp.where(quarter == 0, 1.0, jnp.where(quarter == 2, -1.0, 0.0)).astype(BF16)
    imag4 = jnp.where(quarter == 1, 1.0, jnp.where(quarter == 3, -1.0, 0.0)).astype(BF16)
    sign2 = jnp.where((quarter & 1) == 0, 1.0, -1.0).astype(BF16)
    for t in range(BLOCK // 16):
        x, y = [], []
        for i in (2 * t, 2 * t + 1):
            c = jnp.broadcast_to(angle_ref[0, pl.ds(i, 1)], (8, BLOCK))
            s = jnp.broadcast_to(angle_ref[1, pl.ds(i, 1)], (8, BLOCK))
            x.append(c * same_c + s * same_s)
            y.append(c * next_c + s * next_s)
        x, y = jnp.concatenate(x, axis=0), jnp.concatenate(y, axis=0)
        for c, (u, v) in enumerate(((x, y), (x * cos8 + y * sin8, y * cos8 - x * sin8))):
            u, v = u.astype(BF16), v.astype(BF16)
            turned = u * real4 + v * imag4
            for step, value in ((c, u), (c + 2, turned), (c + 4, u * sign2), (c + 6, turned * sign2)):
                table_ref[pl.ds(step * BLOCK + 16 * t, 16)] = value


def lag_rows(ahead, behind, tail):
    row = iota((LOCAL, 128), 0)
    lane = iota((LOCAL, 128), 1)
    ahead = jnp.where(lane <= row, tail, ahead)
    behind = jnp.where((lane >= 32) & (lane < 64 - row), tail, behind)
    return (
        jnp.take_along_axis(ahead, (lane + row + 1) & 127, axis=1),
        pltpu.roll(behind, 64, 1, stride=1, stride_axis=0),
    )


def front_kernel(
    ahead_count, freq_count, strain_ref, ok_hbm, window_hbm, gath_ref,
    x_ref, ok_ref, window_ref, table_ref, angle_ref, spread_ref, band_ref, white_ref,
    in_sem, small_sem, send_sem, recv_sem,
):
    me = lax.axis_index("ch")
    freq = lax.axis_index("freq")
    first_bin = freq * LOCAL + 1

    small = [
        pltpu.make_async_copy(ok_hbm, ok_ref, small_sem.at[0]),
        pltpu.make_async_copy(window_hbm, window_ref, small_sem.at[1]),
    ]
    for load in small:
        load.start()
    load_strain = pltpu.make_async_copy(strain_ref, x_ref, in_sem)
    load_strain.start()

    core = me % 2
    partner = me + 1 - 2 * core
    exists = lambda other: (other >= 0) & (other < ahead_count)
    barrier = pltpu.get_barrier_semaphore()
    peers = jnp.int32(1)
    pl.semaphore_signal(barrier, 1, device_id={"ch": partner}, device_id_type=MESH)
    for step in (4, -4, 2, -2):
        peers = peers + exists(me + step).astype(jnp.int32)

        @pl.when(exists(me + step))
        def _():
            pl.semaphore_signal(barrier, 1, device_id={"ch": me + step}, device_id_type=MESH)

    write_table(table_ref, angle_ref, first_bin)
    write_spread(spread_ref)
    write_band(band_ref, (freq > 0).astype(F32), (freq < freq_count - 1).astype(F32))

    for slot in range(10, SLOTS):
        gath_ref[slot] = jnp.zeros((TALL, 128), BF16)

    @pl.when((me < AHEAD) | (me >= ahead_count - AHEAD))
    def _():
        for distance in range(1, AHEAD + 1):
            for step, slot in ((distance, SLOT_AHEAD[distance]), (-distance, SLOT_BEHIND[distance])):

                @pl.when((me + step < 0) | (me + step >= ahead_count))
                def _():
                    gath_ref[slot] = jnp.zeros((TALL, 128), BF16)

    for load in small:
        load.wait()
    usable = (window_ref[...].astype(F32) * ok_ref[...].astype(F32)).astype(BF16)
    lane = iota((LOCAL, 128), 1)
    channel = iota((LOCAL, 128), 0)
    for slot, at in ((SLOT_AHEAD[0], channel), (SLOT_BEHIND[0], LOCAL - 1 - channel)):
        spread = jnp.dot(usable, (lane == at).astype(BF16), preferred_element_type=F32)
        gath_ref[slot, pl.ds(4 * LOCAL, WINDOWS)] = spread.astype(BF16)
    keep = []
    for half in range(2):
        expand = (iota((WINDOWS, 128), 0) == 4 * half + iota((WINDOWS, 128), 1) // 32).astype(BF16)
        keep.append(lax.dot_general(usable, expand, (((0,), (0,)), ((), ())), preferred_element_type=F32))

    load_strain.wait()
    spectrum = jnp.zeros((ROWS, BLOCK), F32)
    for block in range(SAMPLES // BLOCK):
        low = max(block * BLOCK - TIME_HALF, 0)
        high = min(block * BLOCK + BLOCK + TIME_HALF, SAMPLES)
        skip = low - (block * BLOCK - TIME_HALF)
        sums = jnp.dot(
            jnp.abs(x_ref[:, low:high]), spread_ref[skip : skip + high - low], preferred_element_type=F32
        )
        level = sums * (1.0 / (2 * TIME_HALF + 1)) + 1e-06
        leveled = (x_ref[:, block * BLOCK : (block + 1) * BLOCK].astype(F32) / level).astype(BF16)
        spectrum = spectrum + jnp.dot(
            leveled, table_ref[block * BLOCK : (block + 1) * BLOCK], preferred_element_type=F32
        )
    power = spectrum * spectrum
    coarse = power.astype(BF16)
    fine = (power - coarse.astype(F32)).astype(BF16)
    smooth = jnp.dot(coarse, band_ref[...], preferred_element_type=F32) + jnp.dot(
        fine, band_ref[...], preferred_element_type=F32
    )
    white_ref[...] = spectrum[:, :128] * lax.rsqrt(smooth * (1.0 / (2 * BIN_HALF + 1)) + 1e-06)
    by_window = [white_ref[pl.ds(w, LOCAL, stride=WINDOWS)] for w in range(WINDOWS)]
    lanes = iota((LOCAL, 128), 1) // 32
    flip = (iota((LOCAL, LOCAL), 0) + iota((LOCAL, LOCAL), 1) == LOCAL - 1).astype(BF16)
    for group in range(GROUPS):
        for half in range(2):
            piece = None
            for i in range(4):
                moved = pltpu.roll(by_window[4 * half + i], (32 * (i - group)) % 128, 1)
                piece = moved if piece is None else jnp.where(lanes == i, moved, piece)
            piece = (piece * keep[half]).astype(BF16)
            where = pl.ds((2 * group + half) * LOCAL, LOCAL)
            gath_ref[SLOT_AHEAD[0], where] = piece
            gath_ref[SLOT_BEHIND[0], where] = jnp.dot(flip, piece, preferred_element_type=F32).astype(BF16)

    pick = lambda even, odd: jnp.where(core == 0, even, odd)

    def copy(src, dst, which, recv, target):
        return pltpu.make_async_remote_copy(
            src_ref=gath_ref.at[src], dst_ref=gath_ref.at[dst], send_sem=send_sem.at[which],
            recv_sem=recv_sem.at[recv], device_id={"ch": target}, device_id_type=MESH,
        )

    own_sends = [
        (SLOT_BEHIND[0], SLOT_BEHIND[4], 7, me + 4),
        (SLOT_AHEAD[0], SLOT_AHEAD[4], 3, me - 4),
        (SLOT_BEHIND[0], SLOT_BEHIND[2], 5, me + 2),
        (SLOT_AHEAD[0], SLOT_AHEAD[2], 1, me - 2),
        (pick(SLOT_BEHIND[0], SLOT_AHEAD[0]), pick(SLOT_BEHIND[1], SLOT_AHEAD[1]), pick(4, 0), partner),
    ]
    passes = [
        (SLOT_BEHIND[2], pick(SLOT_BEHIND[3], SLOT_BEHIND[1]), 5, pick(6, 4), me - 2),
        (SLOT_AHEAD[2], pick(SLOT_AHEAD[1], SLOT_AHEAD[3]), 1, pick(0, 2), me + 2),
        (pick(SLOT_AHEAD[4], SLOT_BEHIND[4]), pick(SLOT_AHEAD[3], SLOT_BEHIND[3]), pick(3, 7), pick(2, 6), me + pick(4, -4)),
    ]
    pl.semaphore_wait(barrier, peers)
    for which, (src, dst, recv, target) in enumerate(own_sends):
        @pl.when(exists(target))
        def _():
            copy(src, dst, which, recv, target).start()
    for i, (src, dst, mine, recv, source) in enumerate(passes):
        @pl.when(exists(source))
        def _():
            copy(src, src, 0, mine, partner).wait_recv()
            copy(src, dst, 5 + i, recv, partner).start()

    for slot, mine, source in (
        (pick(SLOT_BEHIND[4], SLOT_AHEAD[4]), pick(7, 3), me - pick(4, -4)),
        (pick(SLOT_AHEAD[1], SLOT_BEHIND[1]), pick(0, 4), partner),
        (pick(SLOT_BEHIND[1], SLOT_AHEAD[1]), pick(4, 0), me - pick(1, -1)),
        (SLOT_AHEAD[3], 2, me + 3),
        (SLOT_BEHIND[3], 6, me - 3),
    ):
        @pl.when(exists(source))
        def _():
            copy(slot, slot, 0, mine, partner).wait_recv()
    for which, (src, dst, recv, target) in enumerate(own_sends):
        @pl.when(exists(target))
        def _():
            copy(src, dst, which, recv, target).wait_send()
    for i, (src, dst, mine, recv, source) in enumerate(passes):
        @pl.when(exists(source))
        def _():
            copy(src, dst, 5 + i, recv, partner).wait_send()


def front(strain, channel_ok, window_ok, ahead_count, freq_count):
    hbm = pl.BlockSpec(memory_space=pltpu.MemorySpace.HBM)
    vmem = pl.BlockSpec(memory_space=pltpu.VMEM)
    args = (strain.reshape(ROWS, SAMPLES), channel_ok.reshape(1, LOCAL), window_ok.T)
    return pl.pallas_call(
        functools.partial(front_kernel, ahead_count, freq_count),
        out_shape=jax.ShapeDtypeStruct((SLOTS, TALL, 128), BF16),
        in_specs=[hbm, hbm, hbm],
        out_specs=vmem,
        scratch_shapes=[
            pltpu.VMEM((ROWS, SAMPLES), BF16),
            pltpu.VMEM((1, LOCAL), jnp.int32),
            pltpu.VMEM((WINDOWS, LOCAL), jnp.int32),
            pltpu.VMEM((SAMPLES, BLOCK), BF16),
            pltpu.VMEM((2, 40, BLOCK), F32),
            pltpu.VMEM((2 * BLOCK, BLOCK), BF16),
            pltpu.VMEM((BLOCK, 128), BF16),
            pltpu.VMEM((ROWS, 128), F32),
            pltpu.SemaphoreType.DMA,
            pltpu.SemaphoreType.DMA((2,)),
            pltpu.SemaphoreType.DMA((8,)),
            pltpu.SemaphoreType.DMA((8,)),
        ],
        compiler_params=pltpu.CompilerParams(collective_id=0, has_side_effects=True, vmem_limit_bytes=VMEM_LIMIT),
        name="front",
    )(*(pltpu.with_memory_space_constraint(arg, pltpu.HBM) for arg in args))


def cross_kernel(gath_ref, ahead_hbm, behind_hbm, ahead_ref, behind_ref, out_sem):
    contract = (((1,), (1,)), ((), ()))
    per_step = LOCAL // STEPS
    use = [gath_ref[slot, pl.ds(4 * LOCAL, WINDOWS)].astype(F32) for slot in range(10)]
    beside = []
    for tile in range(3):
        moved = [pltpu.roll(use[slot], LOCAL * (slot % 4), 1) for slot in range(4 * tile, min(4 * tile + 4, 10))]
        beside.append(functools.reduce(jnp.add, moved).astype(BF16))
    pairs = lax.dot_general(
        use[0][:, :LOCAL].astype(BF16), jnp.concatenate(beside, axis=1), (((0,), (0,)), ((), ())), preferred_element_type=F32
    )
    scales = [1.0 / jnp.maximum(n, 1.0) for n in lag_rows(pairs[:, :128], pairs[:, 128:256], pairs[:, 256:])]
    lane_of = iota((LOCAL, 256), 1) % 16
    imaginary = (iota((LOCAL, 256), 1) // 16) % 2 == 1
    copies = []
    for step in range(STEPS):
        group, first = divmod(step * per_step, 16)
        low, high = (pl.ds((2 * group + half) * LOCAL, LOCAL) for half in range(2))
        own = jnp.concatenate([gath_ref[0, low], gath_ref[0, high]], axis=1)
        wide = own.astype(F32)
        swap = jnp.where(imaginary, pltpu.roll(wide, 16, 1), -pltpu.roll(wide, 240, 1)).astype(BF16)
        lhs = jnp.concatenate(
            [
                jnp.where(lane_of == first + f, value, jnp.zeros_like(value))
                for value in (own, swap)
                for f in range(per_step)
            ],
            axis=0,
        )
        rhs = jnp.concatenate([gath_ref[:, part].reshape(SLOTS * LOCAL, 128) for part in (low, high)], axis=1)
        cross = lax.dot_general(lhs, rhs, contract, preferred_element_type=F32)
        for part in range(2):
            for f in range(per_step):
                rows = slice((part * per_step + f) * LOCAL, (part * per_step + f + 1) * LOCAL)
                ahead, behind = lag_rows(cross[rows, :128], cross[rows, 128:256], cross[rows, 256:])
                ahead_ref[part, step * per_step + f] = (ahead * scales[0]).astype(BF16)
                behind_ref[part, step * per_step + f] = (behind * scales[1]).astype(BF16)
        done = pl.ds(step * per_step, per_step)
        for side, (src, dst) in enumerate(((ahead_ref, ahead_hbm), (behind_ref, behind_hbm))):
            copies.append(pltpu.make_async_copy(src.at[:, done], dst.at[:, done], out_sem.at[side, step]))
            copies[-1].start()
    for copy in copies:
        copy.wait()


def cross(gathered):
    shape = (2, LOCAL, LOCAL, REACH)
    vmem = pl.BlockSpec(memory_space=pltpu.VMEM)
    hbm = pl.BlockSpec(memory_space=pltpu.MemorySpace.HBM)
    return pl.pallas_call(
        cross_kernel,
        out_shape=(jax.ShapeDtypeStruct(shape, BF16), jax.ShapeDtypeStruct(shape, BF16)),
        in_specs=[vmem],
        out_specs=(hbm, hbm),
        scratch_shapes=[pltpu.VMEM(shape, BF16), pltpu.VMEM(shape, BF16), pltpu.SemaphoreType.DMA((2, STEPS))],
        compiler_params=pltpu.CompilerParams(vmem_limit_bytes=VMEM_LIMIT),
        name="cross",
    )(gathered)


def solution(mesh):
    ahead_count = mesh.shape["ch"]
    freq_count = mesh.shape["freq"]

    def per_device(strain, channel_ok, window_ok):
        gathered = front(strain, channel_ok, window_ok, ahead_count, freq_count)
        return cross(gathered)

    return jax.shard_map(
        per_device,
        mesh=mesh,
        in_specs=(P("ch", None, None), P("ch"), P("ch", None)),
        out_specs=(P(None, "freq", "ch", None), P(None, "freq", "ch", None)),
        check_vma=False,
    )
```

```python
import functools
import math

import jax
import jax.numpy as jnp
from jax import lax
from jax.experimental import pallas as pl
from jax.experimental.pallas import tpu as pltpu
from jax.sharding import PartitionSpec as P

WINDOWS = 8
SAMPLES = 2048
REACH = 128
TIME_HALF = 128
BIN_HALF = 32
LOCAL = 32
AHEAD = REACH // LOCAL
BLOCK = 256
ROWS = LOCAL * WINDOWS
GROUPS = 2
RING = 16
TALL = 4 * LOCAL + WINDOWS
VMEM_LIMIT = 24 << 20
STEPS = 4
F32 = jnp.float32
BF16 = jnp.bfloat16
MESH = pl.DeviceIdType.MESH

SLOT_AHEAD = (0, 1, 2, 3, 8)
SLOT_BEHIND = (5, 6, 7, 4, 9)
SLOTS = 12


def iota(shape, axis):
    return lax.broadcasted_iota(jnp.int32, shape, axis)


def cos_sin(index):
    quarter = SAMPLES // 4
    turn = (index + quarter // 2) // quarter
    x = (index - turn * quarter).astype(F32) * (2.0 * math.pi / SAMPLES)
    y = x * x
    s = x * (1.0 + y * (-1 / 6 + y * (1 / 120 + y * (-1 / 5040 + y * (1 / 362880)))))
    c = 1.0 + y * (-1 / 2 + y * (1 / 24 + y * (-1 / 720 + y * (1 / 40320))))
    turn = turn & 3
    odd = (turn & 1) == 1
    cos = jnp.where(odd, s, c)
    sin = jnp.where(odd, c, s)
    cos = jnp.where((turn == 1) | (turn == 2), -cos, cos)
    sin = jnp.where(turn >= 2, -sin, sin)
    return cos, sin


def lane_bin(lane):
    block = lane // 64
    within = (lane // 32) % 2 * 16 + lane % 16
    return within + jnp.where(block == 1, -LOCAL, jnp.where(block == 2, LOCAL, 0))


def write_spread(spread_ref):
    half = BLOCK // 2
    row, lane = iota((half, half), 0), iota((half, half), 1)
    lower = (row >= lane).astype(BF16)
    upper = (row <= lane).astype(BF16)
    ones = jnp.ones((half, half), BF16)
    zeros = jnp.zeros((half, half), BF16)
    for i, pair in enumerate(((lower, zeros), (ones, lower), (upper, ones), (zeros, upper))):
        for j, piece in enumerate(pair):
            spread_ref[i * half : (i + 1) * half, j * half : (j + 1) * half] = piece


def write_band(band_ref, below, above):
    shape = (16, 128)
    target = iota(shape, 1) // 32 % 2 * 16 + iota(shape, 1) % 16
    for group in range(GROUPS):
        source = iota(shape, 0) + 16 * group
        pieces = (
            jnp.ones(shape, BF16),
            jnp.where(source >= target, below, 0.0).astype(BF16),
            jnp.where(source <= target, above, 0.0).astype(BF16),
            jnp.zeros(shape, BF16),
        )
        for block, piece in enumerate(pieces):
            for part in range(2):
                band_ref[pl.ds(block * 64 + group * 32 + part * 16, 16)] = piece


def table_parts(angle_ref, first_bin):
    row = iota((48, BLOCK), 0)
    step_of = jnp.where(row < 32, 8 * row, jnp.where(row < 40, row - 32, 256 * (row - 40)))
    bin_of = lane_bin(iota((48, BLOCK), 1)) + first_bin
    cos, sin = cos_sin((bin_of * step_of) & (SAMPLES - 1))
    scale = 1.0 / math.sqrt(SAMPLES)
    angle_ref[0] = cos[:32] * scale
    angle_ref[1] = sin[:32] * scale
    imaginary = (iota((8, BLOCK), 1) // 16) % 2 == 1
    cos1, sin1 = cos[32:40], sin[32:40]
    same_c, same_s = jnp.where(imaginary, -sin1, cos1), jnp.where(imaginary, -cos1, -sin1)
    cos8 = jnp.broadcast_to(cos[41:42], (16, BLOCK))
    sin8 = jnp.broadcast_to(sin[41:42], (16, BLOCK))
    quarter = (lane_bin(iota((16, BLOCK), 1)) + first_bin) & 3
    real4 = jnp.where(quarter == 0, 1.0, jnp.where(quarter == 2, -1.0, 0.0)).astype(BF16)
    imag4 = jnp.where(quarter == 1, 1.0, jnp.where(quarter == 3, -1.0, 0.0)).astype(BF16)
    sign2 = jnp.where((quarter & 1) == 0, 1.0, -1.0).astype(BF16)
    return same_c, same_s, cos8, sin8, real4, imag4, sign2


def write_table(table_ref, angle_ref, parts, odd):
    same_c, same_s, cos8, sin8, real4, imag4, sign2 = parts
    next_c, next_s = same_s, -same_c
    for t in range(BLOCK // 16):
        x, y = [], []
        for i in (2 * t, 2 * t + 1):
            c = jnp.broadcast_to(angle_ref[0, pl.ds(i, 1)], (8, BLOCK))
            s = jnp.broadcast_to(angle_ref[1, pl.ds(i, 1)], (8, BLOCK))
            x.append(c * same_c + s * same_s)
            y.append(c * next_c + s * next_s)
        x, y = jnp.concatenate(x, axis=0), jnp.concatenate(y, axis=0)
        if odd:
            x, y = x * cos8 + y * sin8, y * cos8 - x * sin8
        u, v = x.astype(BF16), y.astype(BF16)
        turned = u * real4 + v * imag4
        for step, value in ((0, u), (2, turned), (4, u * sign2), (6, turned * sign2)):
            table_ref[pl.ds((step + odd) * BLOCK + 16 * t, 16)] = value


def lag_rows(ahead, behind, tail):
    row = iota((LOCAL, 128), 0)
    lane = iota((LOCAL, 128), 1)
    ahead = jnp.where(lane <= row, tail, ahead)
    behind = jnp.where((lane >= 32) & (lane < 64 - row), tail, behind)
    reverse = 7 - iota((8, 128), 0)
    turned = []
    for at in range(0, LOCAL, 8):
        rows = jnp.take_along_axis(ahead[at : at + 8], reverse, axis=0)
        rows = pltpu.roll(rows, 120 - at, 1, stride=1, stride_axis=0)
        turned.append(jnp.take_along_axis(rows, reverse, axis=0))
    return jnp.concatenate(turned, axis=0), pltpu.roll(behind, 64, 1, stride=1, stride_axis=0)


def front_kernel(
    ahead_count, freq_count, strain_ref, ok_hbm, window_hbm, gath_ref,
    x_ref, ok_ref, window_ref, table_ref, angle_ref, spread_ref, band_ref, white_ref,
    in_sem, small_sem, send_sem, recv_sem,
):
    me = lax.axis_index("ch")
    freq = lax.axis_index("freq")
    first_bin = freq * LOCAL + 1

    small = [
        pltpu.make_async_copy(ok_hbm, ok_ref, small_sem.at[0]),
        pltpu.make_async_copy(window_hbm, window_ref, small_sem.at[1]),
    ]
    for load in small:
        load.start()
    load_strain = pltpu.make_async_copy(strain_ref, x_ref, in_sem)
    load_strain.start()

    core = me % 2
    partner = me + 1 - 2 * core
    exists = lambda other: (other >= 0) & (other < ahead_count)
    pick = lambda even, odd: jnp.where(core == 0, even, odd)
    far = pick(-3, 3)
    straight = lambda other: exists(other) & (other // RING == me // RING)
    barrier = pltpu.get_barrier_semaphore()
    peers = jnp.int32(1)
    pl.semaphore_signal(barrier, 1, device_id={"ch": partner}, device_id_type=MESH)
    for step, there in (
        (4, exists(me + 4)), (-4, exists(me - 4)), (far, straight(me + far)), (2, exists(me + 2)), (-2, exists(me - 2))
    ):
        peers = peers + there.astype(jnp.int32)

        @pl.when(there)
        def _():
            pl.semaphore_signal(barrier, 1, device_id={"ch": me + step}, device_id_type=MESH)

    parts = table_parts(angle_ref, first_bin)
    write_table(table_ref, angle_ref, parts, 0)
    write_spread(spread_ref)
    write_band(band_ref, (freq > 0).astype(F32), (freq < freq_count - 1).astype(F32))

    for slot in range(10, SLOTS):
        gath_ref[slot] = jnp.zeros((TALL, 128), BF16)

    @pl.when((me < AHEAD) | (me >= ahead_count - AHEAD))
    def _():
        for distance in range(1, AHEAD + 1):
            for step, slot in ((distance, SLOT_AHEAD[distance]), (-distance, SLOT_BEHIND[distance])):

                @pl.when((me + step < 0) | (me + step >= ahead_count))
                def _():
                    gath_ref[slot] = jnp.zeros((TALL, 128), BF16)

    for load in small:
        load.wait()
    usable = (window_ref[...].astype(F32) * ok_ref[...].astype(F32)).astype(BF16)
    lane = iota((LOCAL, 128), 1)
    channel = iota((LOCAL, 128), 0)
    for slot, at in ((SLOT_AHEAD[0], channel), (SLOT_BEHIND[0], LOCAL - 1 - channel)):
        spread = jnp.dot(usable, (lane == at).astype(BF16), preferred_element_type=F32)
        gath_ref[slot, pl.ds(4 * LOCAL, WINDOWS)] = spread.astype(BF16)
    keep = []
    for half in range(2):
        expand = (iota((WINDOWS, 128), 0) == 4 * half + iota((WINDOWS, 128), 1) // 32).astype(BF16)
        keep.append(lax.dot_general(usable, expand, (((0,), (0,)), ((), ())), preferred_element_type=F32))

    load_strain.wait()
    write_table(table_ref, angle_ref, parts, 1)
    spectrum = jnp.zeros((ROWS, BLOCK), F32)
    for block in (0, 2, 4, 6, 1, 3, 5, 7):
        low = max(block * BLOCK - TIME_HALF, 0)
        high = min(block * BLOCK + BLOCK + TIME_HALF, SAMPLES)
        skip = low - (block * BLOCK - TIME_HALF)
        sums = jnp.dot(
            jnp.abs(x_ref[:, low:high]), spread_ref[skip : skip + high - low], preferred_element_type=F32
        )
        level = sums * (1.0 / (2 * TIME_HALF + 1)) + 1e-06
        leveled = (x_ref[:, block * BLOCK : (block + 1) * BLOCK].astype(F32) / level).astype(BF16)
        spectrum = spectrum + jnp.dot(
            leveled, table_ref[block * BLOCK : (block + 1) * BLOCK], preferred_element_type=F32
        )
    power = spectrum * spectrum
    coarse = power.astype(BF16)
    fine = (power - coarse.astype(F32)).astype(BF16)
    smooth = jnp.dot(coarse, band_ref[...], preferred_element_type=F32) + jnp.dot(
        fine, band_ref[...], preferred_element_type=F32
    )
    white_ref[...] = spectrum[:, :128] * lax.rsqrt(smooth * (1.0 / (2 * BIN_HALF + 1)) + 1e-06)
    by_window = [white_ref[pl.ds(w, LOCAL, stride=WINDOWS)] for w in range(WINDOWS)]
    lanes = iota((LOCAL, 128), 1) // 32
    reverse = 7 - iota((8, 128), 0)
    for group in range(GROUPS):
        for half in range(2):
            piece = None
            for i in range(4):
                moved = pltpu.roll(by_window[4 * half + i], (32 * (i - group)) % 128, 1)
                piece = moved if piece is None else jnp.where(lanes == i, moved, piece)
            piece = piece * keep[half]
            where = pl.ds((2 * group + half) * LOCAL, LOCAL)
            flipped = [jnp.take_along_axis(piece[at : at + 8], reverse, axis=0) for at in range(LOCAL - 8, -1, -8)]
            gath_ref[SLOT_AHEAD[0], where] = piece.astype(BF16)
            gath_ref[SLOT_BEHIND[0], where] = jnp.concatenate(flipped, axis=0).astype(BF16)

    def copy(src, dst, which, recv, target):
        return pltpu.make_async_remote_copy(
            src_ref=gath_ref.at[src], dst_ref=gath_ref.at[dst], send_sem=send_sem.at[which],
            recv_sem=recv_sem.at[recv], device_id={"ch": target}, device_id_type=MESH,
        )

    own_sends = [
        (SLOT_BEHIND[0], SLOT_BEHIND[4], 7, me + 4, exists(me + 4)),
        (SLOT_AHEAD[0], SLOT_AHEAD[4], 3, me - 4, exists(me - 4)),
        (pick(SLOT_AHEAD[0], SLOT_BEHIND[0]), pick(SLOT_AHEAD[3], SLOT_BEHIND[3]), pick(2, 6), me + far, straight(me + far)),
        (SLOT_BEHIND[0], SLOT_BEHIND[2], 5, me + 2, exists(me + 2)),
        (SLOT_AHEAD[0], SLOT_AHEAD[2], 1, me - 2, exists(me - 2)),
        (pick(SLOT_BEHIND[0], SLOT_AHEAD[0]), pick(SLOT_BEHIND[1], SLOT_AHEAD[1]), pick(4, 0), partner, True),
    ]
    own_sends = own_sends[3:5] + own_sends[:3] + own_sends[5:]
    beyond = me + pick(4, -4)
    passes = [
        (SLOT_BEHIND[2], pick(SLOT_BEHIND[3], SLOT_BEHIND[1]), 5, pick(6, 4), exists(me - 2)),
        (SLOT_AHEAD[2], pick(SLOT_AHEAD[1], SLOT_AHEAD[3]), 1, pick(0, 2), exists(me + 2)),
        (
            pick(SLOT_AHEAD[4], SLOT_BEHIND[4]), pick(SLOT_AHEAD[3], SLOT_BEHIND[3]), pick(3, 7), pick(2, 6),
            exists(beyond) & ~straight(beyond),
        ),
    ]
    pl.semaphore_wait(barrier, peers)
    for which, (src, dst, recv, target, there) in enumerate(own_sends):
        @pl.when(there)
        def _():
            copy(src, dst, which, recv, target).start()
    for i, (src, dst, mine, recv, there) in enumerate(passes):
        @pl.when(there)
        def _():
            copy(src, src, 0, mine, partner).wait_recv()
            copy(src, dst, 6 + i, recv, partner).start()

    for slot, mine, there in (
        (pick(SLOT_AHEAD[4], SLOT_BEHIND[4]), pick(3, 7), straight(beyond)),
        (pick(SLOT_BEHIND[4], SLOT_AHEAD[4]), pick(7, 3), exists(me - pick(4, -4))),
        (pick(SLOT_AHEAD[1], SLOT_BEHIND[1]), pick(0, 4), True),
        (pick(SLOT_BEHIND[1], SLOT_AHEAD[1]), pick(4, 0), exists(me - pick(1, -1))),
        (SLOT_AHEAD[3], 2, exists(me + 3)),
        (SLOT_BEHIND[3], 6, exists(me - 3)),
    ):
        @pl.when(there)
        def _():
            copy(slot, slot, 0, mine, partner).wait_recv()
    for which, (src, dst, recv, target, there) in enumerate(own_sends):
        @pl.when(there)
        def _():
            copy(src, dst, which, recv, target).wait_send()
    for i, (src, dst, mine, recv, there) in enumerate(passes):
        @pl.when(there)
        def _():
            copy(src, dst, 6 + i, recv, partner).wait_send()


def front(strain, channel_ok, window_ok, ahead_count, freq_count):
    hbm = pl.BlockSpec(memory_space=pltpu.MemorySpace.HBM)
    vmem = pl.BlockSpec(memory_space=pltpu.VMEM)
    args = (strain.reshape(ROWS, SAMPLES), channel_ok.reshape(1, LOCAL), window_ok.T)
    return pl.pallas_call(
        functools.partial(front_kernel, ahead_count, freq_count),
        out_shape=jax.ShapeDtypeStruct((SLOTS, TALL, 128), BF16),
        in_specs=[hbm, hbm, hbm],
        out_specs=vmem,
        scratch_shapes=[
            pltpu.VMEM((ROWS, SAMPLES), BF16),
            pltpu.VMEM((1, LOCAL), jnp.int32),
            pltpu.VMEM((WINDOWS, LOCAL), jnp.int32),
            pltpu.VMEM((SAMPLES, BLOCK), BF16),
            pltpu.VMEM((2, 32, BLOCK), F32),
            pltpu.VMEM((2 * BLOCK, BLOCK), BF16),
            pltpu.VMEM((BLOCK, 128), BF16),
            pltpu.VMEM((ROWS, 128), F32),
            pltpu.SemaphoreType.DMA,
            pltpu.SemaphoreType.DMA((2,)),
            pltpu.SemaphoreType.DMA((9,)),
            pltpu.SemaphoreType.DMA((8,)),
        ],
        compiler_params=pltpu.CompilerParams(collective_id=0, has_side_effects=True, vmem_limit_bytes=VMEM_LIMIT),
        name="front",
    )(*(pltpu.with_memory_space_constraint(arg, pltpu.HBM) for arg in args))


def cross_kernel(gath_ref, ahead_hbm, behind_hbm, ahead_ref, behind_ref, out_sem):
    contract = (((1,), (1,)), ((), ()))
    per_step = LOCAL // STEPS
    use = [gath_ref[slot, pl.ds(4 * LOCAL, WINDOWS)].astype(F32) for slot in range(10)]
    beside = []
    for tile in range(3):
        moved = [pltpu.roll(use[slot], LOCAL * (slot % 4), 1) for slot in range(4 * tile, min(4 * tile + 4, 10))]
        beside.append(functools.reduce(jnp.add, moved).astype(BF16))
    pairs = lax.dot_general(
        use[0][:, :LOCAL].astype(BF16), jnp.concatenate(beside, axis=1), (((0,), (0,)), ((), ())), preferred_element_type=F32
    )
    scales = [1.0 / jnp.maximum(n, 1.0) for n in lag_rows(pairs[:, :128], pairs[:, 128:256], pairs[:, 256:])]
    lane_of = iota((LOCAL, 256), 1) % 16
    imaginary = (iota((LOCAL, 256), 1) // 16) % 2 == 1
    copies = []
    for step in range(STEPS):
        group, first = divmod(step * per_step, 16)
        low, high = (pl.ds((2 * group + half) * LOCAL, LOCAL) for half in range(2))
        own = jnp.concatenate([gath_ref[0, low], gath_ref[0, high]], axis=1)
        wide = own.astype(F32)
        swap = jnp.where(imaginary, pltpu.roll(wide, 16, 1), -pltpu.roll(wide, 240, 1)).astype(BF16)
        lhs = jnp.concatenate(
            [
                jnp.where(lane_of == first + f, value, jnp.zeros_like(value))
                for value in (own, swap)
                for f in range(per_step)
            ],
            axis=0,
        )
        rhs = jnp.concatenate([gath_ref[:, part].reshape(SLOTS * LOCAL, 128) for part in (low, high)], axis=1)
        cross = lax.dot_general(lhs, rhs, contract, preferred_element_type=F32)
        for part in range(2):
            for f in range(per_step):
                rows = slice((part * per_step + f) * LOCAL, (part * per_step + f + 1) * LOCAL)
                ahead, behind = lag_rows(cross[rows, :128], cross[rows, 128:256], cross[rows, 256:])
                ahead_ref[part, step * per_step + f] = (ahead * scales[0]).astype(BF16)
                behind_ref[part, step * per_step + f] = (behind * scales[1]).astype(BF16)
            done = pl.ds(step * per_step, per_step)
            for side, (src, dst) in enumerate(((ahead_ref, ahead_hbm), (behind_ref, behind_hbm))):
                copies.append(
                    pltpu.make_async_copy(src.at[part, done], dst.at[part, done], out_sem.at[side, part, step])
                )
                copies[-1].start()
    for copy in copies:
        copy.wait()


def cross(gathered):
    shape = (2, LOCAL, LOCAL, REACH)
    vmem = pl.BlockSpec(memory_space=pltpu.VMEM)
    hbm = pl.BlockSpec(memory_space=pltpu.MemorySpace.HBM)
    return pl.pallas_call(
        cross_kernel,
        out_shape=(jax.ShapeDtypeStruct(shape, BF16), jax.ShapeDtypeStruct(shape, BF16)),
        in_specs=[vmem],
        out_specs=(hbm, hbm),
        scratch_shapes=[pltpu.VMEM(shape, BF16), pltpu.VMEM(shape, BF16), pltpu.SemaphoreType.DMA((2, 2, STEPS))],
        compiler_params=pltpu.CompilerParams(vmem_limit_bytes=VMEM_LIMIT),
        name="cross",
    )(gathered)


def solution(mesh):
    ahead_count = mesh.shape["ch"]
    freq_count = mesh.shape["freq"]

    def per_device(strain, channel_ok, window_ok):
        gathered = front(strain, channel_ok, window_ok, ahead_count, freq_count)
        return cross(gathered)

    return jax.shard_map(
        per_device,
        mesh=mesh,
        in_specs=(P("ch", None, None), P("ch"), P("ch", None)),
        out_specs=(P(None, "freq", "ch", None), P(None, "freq", "ch", None)),
        check_vma=False,
    )
```

```python
import functools
import math

import jax
import jax.numpy as jnp
from jax import lax
from jax.experimental import pallas as pl
from jax.experimental.pallas import tpu as pltpu
from jax.sharding import PartitionSpec as P

WINDOWS = 8
SAMPLES = 2048
REACH = 128
TIME_HALF = 128
BIN_HALF = 32
LOCAL = 32
AHEAD = REACH // LOCAL
BLOCK = 256
ROWS = LOCAL * WINDOWS
GROUPS = 2
RING = 16
TALL = 4 * LOCAL + WINDOWS
VMEM_LIMIT = 24 << 20
STEPS = 4
F32 = jnp.float32
BF16 = jnp.bfloat16
MESH = pl.DeviceIdType.MESH

SLOT_AHEAD = (0, 1, 2, 3, 8)
SLOT_BEHIND = (5, 6, 7, 4, 9)
SLOTS = 12


def iota(shape, axis):
    return lax.broadcasted_iota(jnp.int32, shape, axis)


def cos_sin(index):
    quarter = SAMPLES // 4
    turn = (index + quarter // 2) // quarter
    x = (index - turn * quarter).astype(F32) * (2.0 * math.pi / SAMPLES)
    y = x * x
    s = x * (1.0 + y * (-1 / 6 + y * (1 / 120 + y * (-1 / 5040 + y * (1 / 362880)))))
    c = 1.0 + y * (-1 / 2 + y * (1 / 24 + y * (-1 / 720 + y * (1 / 40320))))
    turn = turn & 3
    odd = (turn & 1) == 1
    cos = jnp.where(odd, s, c)
    sin = jnp.where(odd, c, s)
    cos = jnp.where((turn == 1) | (turn == 2), -cos, cos)
    sin = jnp.where(turn >= 2, -sin, sin)
    return cos, sin


def lane_bin(lane):
    block = lane // 64
    within = (lane // 32) % 2 * 16 + lane % 16
    return within + jnp.where(block == 1, -LOCAL, jnp.where(block == 2, LOCAL, 0))


def write_spread(spread_ref):
    half = BLOCK // 2
    row, lane = iota((half, half), 0), iota((half, half), 1)
    lower = (row >= lane).astype(BF16)
    upper = (row <= lane).astype(BF16)
    ones = jnp.ones((half, half), BF16)
    zeros = jnp.zeros((half, half), BF16)
    for i, pair in enumerate(((lower, zeros), (ones, lower), (upper, ones), (zeros, upper))):
        for j, piece in enumerate(pair):
            spread_ref[i * half : (i + 1) * half, j * half : (j + 1) * half] = piece


def write_band(band_ref, below, above):
    shape = (16, 128)
    target = iota(shape, 1) // 32 % 2 * 16 + iota(shape, 1) % 16
    for group in range(GROUPS):
        source = iota(shape, 0) + 16 * group
        pieces = (
            jnp.ones(shape, BF16),
            jnp.where(source >= target, below, 0.0).astype(BF16),
            jnp.where(source <= target, above, 0.0).astype(BF16),
            jnp.zeros(shape, BF16),
        )
        for block, piece in enumerate(pieces):
            for part in range(2):
                band_ref[pl.ds(block * 64 + group * 32 + part * 16, 16)] = piece


def table_parts(angle_ref, first_bin):
    row = iota((48, BLOCK), 0)
    step_of = jnp.where(row < 32, 8 * row, jnp.where(row < 40, row - 32, 256 * (row - 40)))
    bin_of = lane_bin(iota((48, BLOCK), 1)) + first_bin
    cos, sin = cos_sin((bin_of * step_of) & (SAMPLES - 1))
    scale = 1.0 / math.sqrt(SAMPLES)
    angle_ref[0] = cos[:32] * scale
    angle_ref[1] = sin[:32] * scale
    imaginary = (iota((8, BLOCK), 1) // 16) % 2 == 1
    cos1, sin1 = cos[32:40], sin[32:40]
    same_c, same_s = jnp.where(imaginary, -sin1, cos1), jnp.where(imaginary, -cos1, -sin1)
    cos8 = jnp.broadcast_to(cos[41:42], (16, BLOCK))
    sin8 = jnp.broadcast_to(sin[41:42], (16, BLOCK))
    quarter = (lane_bin(iota((16, BLOCK), 1)) + first_bin) & 3
    real4 = jnp.where(quarter == 0, 1.0, jnp.where(quarter == 2, -1.0, 0.0)).astype(BF16)
    imag4 = jnp.where(quarter == 1, 1.0, jnp.where(quarter == 3, -1.0, 0.0)).astype(BF16)
    sign2 = jnp.where((quarter & 1) == 0, 1.0, -1.0).astype(BF16)
    return same_c, same_s, cos8, sin8, real4, imag4, sign2


def write_table(table_ref, angle_ref, parts, odd):
    same_c, same_s, cos8, sin8, real4, imag4, sign2 = parts
    next_c, next_s = same_s, -same_c
    for t in range(BLOCK // 16):
        x, y = [], []
        for i in (2 * t, 2 * t + 1):
            c = jnp.broadcast_to(angle_ref[0, pl.ds(i, 1)], (8, BLOCK))
            s = jnp.broadcast_to(angle_ref[1, pl.ds(i, 1)], (8, BLOCK))
            x.append(c * same_c + s * same_s)
            y.append(c * next_c + s * next_s)
        x, y = jnp.concatenate(x, axis=0), jnp.concatenate(y, axis=0)
        if odd:
            x, y = x * cos8 + y * sin8, y * cos8 - x * sin8
        u, v = x.astype(BF16), y.astype(BF16)
        turned = u * real4 + v * imag4
        for step, value in ((0, u), (2, turned), (4, u * sign2), (6, turned * sign2)):
            table_ref[pl.ds((step + odd) * BLOCK + 16 * t, 16)] = value


def lag_rows(ahead, behind, tail):
    row = iota((LOCAL, 128), 0)
    lane = iota((LOCAL, 128), 1)
    ahead = jnp.where(lane <= row, tail, ahead)
    behind = jnp.where((lane >= 32) & (lane < 64 - row), tail, behind)
    reverse = 7 - iota((8, 128), 0)
    turned = []
    for at in range(0, LOCAL, 8):
        rows = jnp.take_along_axis(ahead[at : at + 8], reverse, axis=0)
        rows = pltpu.roll(rows, 120 - at, 1, stride=1, stride_axis=0)
        turned.append(jnp.take_along_axis(rows, reverse, axis=0))
    return jnp.concatenate(turned, axis=0), pltpu.roll(behind, 64, 1, stride=1, stride_axis=0)


def front_kernel(
    ahead_count, freq_count, strain_ref, ok_hbm, window_hbm, gath_ref,
    x_ref, ok_ref, window_ref, table_ref, angle_ref, spread_ref, band_ref, white_ref,
    in_sem, small_sem, send_sem, recv_sem,
):
    me = lax.axis_index("ch")
    freq = lax.axis_index("freq")
    first_bin = freq * LOCAL + 1

    small = [
        pltpu.make_async_copy(ok_hbm, ok_ref, small_sem.at[0]),
        pltpu.make_async_copy(window_hbm, window_ref, small_sem.at[1]),
    ]
    for load in small:
        load.start()
    load_strain = pltpu.make_async_copy(strain_ref, x_ref, in_sem)
    load_strain.start()

    core = me % 2
    partner = me + 1 - 2 * core
    exists = lambda other: (other >= 0) & (other < ahead_count)
    pick = lambda even, odd: jnp.where(core == 0, even, odd)
    far = pick(-3, 3)
    straight = lambda other: exists(other) & (other // RING == me // RING)
    barrier = pltpu.get_barrier_semaphore()
    peers = jnp.int32(1)
    pl.semaphore_signal(barrier, 1, device_id={"ch": partner}, device_id_type=MESH)
    for step, there in (
        (4, exists(me + 4)), (-4, exists(me - 4)), (far, straight(me + far)), (2, exists(me + 2)), (-2, exists(me - 2))
    ):
        peers = peers + there.astype(jnp.int32)

        @pl.when(there)
        def _():
            pl.semaphore_signal(barrier, 1, device_id={"ch": me + step}, device_id_type=MESH)

    parts = table_parts(angle_ref, first_bin)
    write_table(table_ref, angle_ref, parts, 0)
    write_table(table_ref, angle_ref, parts, 1)
    write_spread(spread_ref)
    write_band(band_ref, (freq > 0).astype(F32), (freq < freq_count - 1).astype(F32))

    for slot in range(10, SLOTS):
        gath_ref[slot] = jnp.zeros((TALL, 128), BF16)

    @pl.when((me < AHEAD) | (me >= ahead_count - AHEAD))
    def _():
        for distance in range(1, AHEAD + 1):
            for step, slot in ((distance, SLOT_AHEAD[distance]), (-distance, SLOT_BEHIND[distance])):

                @pl.when((me + step < 0) | (me + step >= ahead_count))
                def _():
                    gath_ref[slot] = jnp.zeros((TALL, 128), BF16)

    for load in small:
        load.wait()
    usable = (window_ref[...].astype(F32) * ok_ref[...].astype(F32)).astype(BF16)
    lane = iota((LOCAL, 128), 1)
    channel = iota((LOCAL, 128), 0)
    for slot, at in ((SLOT_AHEAD[0], channel), (SLOT_BEHIND[0], LOCAL - 1 - channel)):
        spread = jnp.dot(usable, (lane == at).astype(BF16), preferred_element_type=F32)
        gath_ref[slot, pl.ds(4 * LOCAL, WINDOWS)] = spread.astype(BF16)
    keep = []
    for half in range(2):
        expand = (iota((WINDOWS, 128), 0) == 4 * half + iota((WINDOWS, 128), 1) // 32).astype(BF16)
        keep.append(lax.dot_general(usable, expand, (((0,), (0,)), ((), ())), preferred_element_type=F32))

    load_strain.wait()
    def leveled(block):
        low = max(block * BLOCK - TIME_HALF, 0)
        high = min(block * BLOCK + BLOCK + TIME_HALF, SAMPLES)
        skip = low - (block * BLOCK - TIME_HALF)
        sums = jnp.dot(
            jnp.abs(x_ref[:, low:high]), spread_ref[skip : skip + high - low], preferred_element_type=F32
        )
        level = sums * (1.0 / (2 * TIME_HALF + 1)) + 1e-06
        return (x_ref[:, block * BLOCK : (block + 1) * BLOCK].astype(F32) / level).astype(BF16)

    spectrum = jnp.zeros((ROWS, BLOCK), F32)
    for first in (0, 2, 4, 6):
        both = jnp.concatenate([leveled(first), leveled(first + 1)], axis=1)
        spectrum = spectrum + jnp.dot(
            both, table_ref[first * BLOCK : (first + 2) * BLOCK], preferred_element_type=F32
        )
    power = spectrum * spectrum
    smooth = jnp.dot(power.astype(BF16), band_ref[...], preferred_element_type=F32)
    white_ref[...] = spectrum[:, :128] * lax.rsqrt(smooth * (1.0 / (2 * BIN_HALF + 1)) + 1e-06)
    by_window = [white_ref[pl.ds(w, LOCAL, stride=WINDOWS)] for w in range(WINDOWS)]
    lanes = iota((LOCAL, 128), 1) // 32
    reverse = 7 - iota((8, 128), 0)
    for group in range(GROUPS):
        for half in range(2):
            piece = None
            for i in range(4):
                moved = pltpu.roll(by_window[4 * half + i], (32 * (i - group)) % 128, 1)
                piece = moved if piece is None else jnp.where(lanes == i, moved, piece)
            piece = piece * keep[half]
            where = pl.ds((2 * group + half) * LOCAL, LOCAL)
            flipped = [jnp.take_along_axis(piece[at : at + 8], reverse, axis=0) for at in range(LOCAL - 8, -1, -8)]
            gath_ref[SLOT_AHEAD[0], where] = piece.astype(BF16)
            gath_ref[SLOT_BEHIND[0], where] = jnp.concatenate(flipped, axis=0).astype(BF16)

    def copy(src, dst, which, recv, target):
        return pltpu.make_async_remote_copy(
            src_ref=gath_ref.at[src], dst_ref=gath_ref.at[dst], send_sem=send_sem.at[which],
            recv_sem=recv_sem.at[recv], device_id={"ch": target}, device_id_type=MESH,
        )

    own_sends = [
        (SLOT_BEHIND[0], SLOT_BEHIND[4], 7, me + 4, exists(me + 4)),
        (SLOT_AHEAD[0], SLOT_AHEAD[4], 3, me - 4, exists(me - 4)),
        (pick(SLOT_AHEAD[0], SLOT_BEHIND[0]), pick(SLOT_AHEAD[3], SLOT_BEHIND[3]), pick(2, 6), me + far, straight(me + far)),
        (SLOT_BEHIND[0], SLOT_BEHIND[2], 5, me + 2, exists(me + 2)),
        (SLOT_AHEAD[0], SLOT_AHEAD[2], 1, me - 2, exists(me - 2)),
        (pick(SLOT_BEHIND[0], SLOT_AHEAD[0]), pick(SLOT_BEHIND[1], SLOT_AHEAD[1]), pick(4, 0), partner, True),
    ]
    own_sends = own_sends[3:5] + own_sends[:3] + own_sends[5:]
    beyond = me + pick(4, -4)
    passes = [
        (SLOT_BEHIND[2], pick(SLOT_BEHIND[3], SLOT_BEHIND[1]), 5, pick(6, 4), exists(me - 2)),
        (SLOT_AHEAD[2], pick(SLOT_AHEAD[1], SLOT_AHEAD[3]), 1, pick(0, 2), exists(me + 2)),
        (
            pick(SLOT_AHEAD[4], SLOT_BEHIND[4]), pick(SLOT_AHEAD[3], SLOT_BEHIND[3]), pick(3, 7), pick(2, 6),
            exists(beyond) & ~straight(beyond),
        ),
    ]
    pl.semaphore_wait(barrier, peers)
    for which, (src, dst, recv, target, there) in enumerate(own_sends):
        @pl.when(there)
        def _():
            copy(src, dst, which, recv, target).start()
    for i, (src, dst, mine, recv, there) in enumerate(passes):
        @pl.when(there)
        def _():
            copy(src, src, 0, mine, partner).wait_recv()
            copy(src, dst, 6 + i, recv, partner).start()

    for slot, mine, there in (
        (pick(SLOT_AHEAD[4], SLOT_BEHIND[4]), pick(3, 7), straight(beyond)),
        (pick(SLOT_BEHIND[4], SLOT_AHEAD[4]), pick(7, 3), exists(me - pick(4, -4))),
        (pick(SLOT_AHEAD[1], SLOT_BEHIND[1]), pick(0, 4), True),
        (pick(SLOT_BEHIND[1], SLOT_AHEAD[1]), pick(4, 0), exists(me - pick(1, -1))),
        (SLOT_AHEAD[3], 2, exists(me + 3)),
        (SLOT_BEHIND[3], 6, exists(me - 3)),
    ):
        @pl.when(there)
        def _():
            copy(slot, slot, 0, mine, partner).wait_recv()
    for which, (src, dst, recv, target, there) in enumerate(own_sends):
        @pl.when(there)
        def _():
            copy(src, dst, which, recv, target).wait_send()
    for i, (src, dst, mine, recv, there) in enumerate(passes):
        @pl.when(there)
        def _():
            copy(src, dst, 6 + i, recv, partner).wait_send()


def front(strain, channel_ok, window_ok, ahead_count, freq_count):
    hbm = pl.BlockSpec(memory_space=pltpu.MemorySpace.HBM)
    vmem = pl.BlockSpec(memory_space=pltpu.VMEM)
    args = (strain.reshape(ROWS, SAMPLES), channel_ok.reshape(1, LOCAL), window_ok.T)
    return pl.pallas_call(
        functools.partial(front_kernel, ahead_count, freq_count),
        out_shape=jax.ShapeDtypeStruct((SLOTS, TALL, 128), BF16),
        in_specs=[hbm, hbm, hbm],
        out_specs=vmem,
        scratch_shapes=[
            pltpu.VMEM((ROWS, SAMPLES), BF16),
            pltpu.VMEM((1, LOCAL), jnp.int32),
            pltpu.VMEM((WINDOWS, LOCAL), jnp.int32),
            pltpu.VMEM((SAMPLES, BLOCK), BF16),
            pltpu.VMEM((2, 32, BLOCK), F32),
            pltpu.VMEM((2 * BLOCK, BLOCK), BF16),
            pltpu.VMEM((BLOCK, 128), BF16),
            pltpu.VMEM((ROWS, 128), F32),
            pltpu.SemaphoreType.DMA,
            pltpu.SemaphoreType.DMA((2,)),
            pltpu.SemaphoreType.DMA((9,)),
            pltpu.SemaphoreType.DMA((8,)),
        ],
        compiler_params=pltpu.CompilerParams(collective_id=0, has_side_effects=True, vmem_limit_bytes=VMEM_LIMIT),
        name="front",
    )(*(pltpu.with_memory_space_constraint(arg, pltpu.HBM) for arg in args))


def cross_kernel(gath_ref, ahead_hbm, behind_hbm, ahead_ref, behind_ref, out_sem):
    contract = (((1,), (1,)), ((), ()))
    per_step = LOCAL // STEPS
    use = [gath_ref[slot, pl.ds(4 * LOCAL, WINDOWS)].astype(F32) for slot in range(10)]
    beside = []
    for tile in range(3):
        moved = [pltpu.roll(use[slot], LOCAL * (slot % 4), 1) for slot in range(4 * tile, min(4 * tile + 4, 10))]
        beside.append(functools.reduce(jnp.add, moved).astype(BF16))
    pairs = lax.dot_general(
        use[0][:, :LOCAL].astype(BF16), jnp.concatenate(beside, axis=1), (((0,), (0,)), ((), ())), preferred_element_type=F32
    )
    scales = [1.0 / jnp.maximum(n, 1.0) for n in lag_rows(pairs[:, :128], pairs[:, 128:256], pairs[:, 256:])]
    lane_of = iota((LOCAL, 256), 1) % 16
    imaginary = (iota((LOCAL, 256), 1) // 16) % 2 == 1
    copies = []
    for step in range(STEPS):
        group, first = divmod(step * per_step, 16)
        low, high = (pl.ds((2 * group + half) * LOCAL, LOCAL) for half in range(2))
        own = jnp.concatenate([gath_ref[0, low], gath_ref[0, high]], axis=1)
        wide = own.astype(F32)
        swap = jnp.where(imaginary, pltpu.roll(wide, 16, 1), -pltpu.roll(wide, 240, 1)).astype(BF16)
        lhs = jnp.concatenate(
            [
                jnp.where(lane_of == first + f, value, jnp.zeros_like(value))
                for value in (own, swap)
                for f in range(per_step)
            ],
            axis=0,
        )
        rhs = jnp.concatenate([gath_ref[:, part].reshape(SLOTS * LOCAL, 128) for part in (low, high)], axis=1)
        cross = lax.dot_general(lhs, rhs, contract, preferred_element_type=F32)
        for part in range(2):
            for f in range(per_step):
                rows = slice((part * per_step + f) * LOCAL, (part * per_step + f + 1) * LOCAL)
                ahead, behind = lag_rows(cross[rows, :128], cross[rows, 128:256], cross[rows, 256:])
                ahead_ref[part, step * per_step + f] = (ahead * scales[0]).astype(BF16)
                behind_ref[part, step * per_step + f] = (behind * scales[1]).astype(BF16)
            done = pl.ds(step * per_step, per_step)
            for side, (src, dst) in enumerate(((ahead_ref, ahead_hbm), (behind_ref, behind_hbm))):
                copies.append(
                    pltpu.make_async_copy(src.at[part, done], dst.at[part, done], out_sem.at[side, part, step])
                )
                copies[-1].start()
    for copy in copies:
        copy.wait()


def cross(gathered):
    shape = (2, LOCAL, LOCAL, REACH)
    vmem = pl.BlockSpec(memory_space=pltpu.VMEM)
    hbm = pl.BlockSpec(memory_space=pltpu.MemorySpace.HBM)
    return pl.pallas_call(
        cross_kernel,
        out_shape=(jax.ShapeDtypeStruct(shape, BF16), jax.ShapeDtypeStruct(shape, BF16)),
        in_specs=[vmem],
        out_specs=(hbm, hbm),
        scratch_shapes=[pltpu.VMEM(shape, BF16), pltpu.VMEM(shape, BF16), pltpu.SemaphoreType.DMA((2, 2, STEPS))],
        compiler_params=pltpu.CompilerParams(vmem_limit_bytes=VMEM_LIMIT),
        name="cross",
    )(gathered)


def solution(mesh):
    ahead_count = mesh.shape["ch"]
    freq_count = mesh.shape["freq"]

    def per_device(strain, channel_ok, window_ok):
        gathered = front(strain, channel_ok, window_ok, ahead_count, freq_count)
        return cross(gathered)

    return jax.shard_map(
        per_device,
        mesh=mesh,
        in_specs=(P("ch", None, None), P("ch"), P("ch", None)),
        out_specs=(P(None, "freq", "ch", None), P(None, "freq", "ch", None)),
        check_vma=False,
    )
```

```python
import functools
import math

import jax
import jax.numpy as jnp
from jax import lax
from jax.experimental import pallas as pl
from jax.experimental.pallas import tpu as pltpu
from jax.sharding import PartitionSpec as P

WINDOWS = 8
SAMPLES = 2048
REACH = 128
TIME_HALF = 128
BIN_HALF = 32
LOCAL = 32
AHEAD = REACH // LOCAL
BLOCK = 256
ROWS = LOCAL * WINDOWS
GROUPS = 2
RING = 16
TALL = 4 * LOCAL + WINDOWS
VMEM_LIMIT = 24 << 20
STEPS = 4
F32 = jnp.float32
BF16 = jnp.bfloat16
MESH = pl.DeviceIdType.MESH

SLOT_AHEAD = (0, 1, 2, 3, 8)
SLOT_BEHIND = (5, 6, 7, 4, 9)
SLOTS = 12


def iota(shape, axis):
    return lax.broadcasted_iota(jnp.int32, shape, axis)


def cos_sin(index):
    quarter = SAMPLES // 4
    turn = (index + quarter // 2) // quarter
    x = (index - turn * quarter).astype(F32) * (2.0 * math.pi / SAMPLES)
    y = x * x
    s = x * (1.0 + y * (-1 / 6 + y * (1 / 120 + y * (-1 / 5040 + y * (1 / 362880)))))
    c = 1.0 + y * (-1 / 2 + y * (1 / 24 + y * (-1 / 720 + y * (1 / 40320))))
    turn = turn & 3
    odd = (turn & 1) == 1
    cos = jnp.where(odd, s, c)
    sin = jnp.where(odd, c, s)
    cos = jnp.where((turn == 1) | (turn == 2), -cos, cos)
    sin = jnp.where(turn >= 2, -sin, sin)
    return cos, sin


def lane_bin(lane):
    block = lane // 64
    within = (lane // 32) % 2 * 16 + lane % 16
    return within + jnp.where(block == 1, -LOCAL, jnp.where(block == 2, LOCAL, 0))


def write_spread(spread_ref):
    half = BLOCK // 2
    row, lane = iota((half, half), 0), iota((half, half), 1)
    lower = (row >= lane).astype(BF16)
    upper = (row <= lane).astype(BF16)
    ones = jnp.ones((half, half), BF16)
    zeros = jnp.zeros((half, half), BF16)
    for i, pair in enumerate(((lower, zeros), (ones, lower), (upper, ones), (zeros, upper))):
        for j, piece in enumerate(pair):
            spread_ref[i * half : (i + 1) * half, j * half : (j + 1) * half] = piece


def write_band(band_ref, below, above):
    shape = (16, 128)
    target = iota(shape, 1) // 32 % 2 * 16 + iota(shape, 1) % 16
    for group in range(GROUPS):
        source = iota(shape, 0) + 16 * group
        pieces = (
            jnp.ones(shape, BF16),
            jnp.where(source >= target, below, 0.0).astype(BF16),
            jnp.where(source <= target, above, 0.0).astype(BF16),
            jnp.zeros(shape, BF16),
        )
        for block, piece in enumerate(pieces):
            for part in range(2):
                band_ref[pl.ds(block * 64 + group * 32 + part * 16, 16)] = piece


def table_parts(angle_ref, first_bin):
    row = iota((48, BLOCK), 0)
    step_of = jnp.where(row < 32, 8 * row, jnp.where(row < 40, row - 32, 256 * (row - 40)))
    bin_of = lane_bin(iota((48, BLOCK), 1)) + first_bin
    cos, sin = cos_sin((bin_of * step_of) & (SAMPLES - 1))
    scale = 1.0 / math.sqrt(SAMPLES)
    angle_ref[0] = cos[:32] * scale
    angle_ref[1] = sin[:32] * scale
    imaginary = (iota((8, BLOCK), 1) // 16) % 2 == 1
    cos1, sin1 = cos[32:40], sin[32:40]
    same_c, same_s = jnp.where(imaginary, -sin1, cos1), jnp.where(imaginary, -cos1, -sin1)
    cos8 = jnp.broadcast_to(cos[41:42], (16, BLOCK))
    sin8 = jnp.broadcast_to(sin[41:42], (16, BLOCK))
    quarter = (lane_bin(iota((16, BLOCK), 1)) + first_bin) & 3
    real4 = jnp.where(quarter == 0, 1.0, jnp.where(quarter == 2, -1.0, 0.0)).astype(BF16)
    imag4 = jnp.where(quarter == 1, 1.0, jnp.where(quarter == 3, -1.0, 0.0)).astype(BF16)
    sign2 = jnp.where((quarter & 1) == 0, 1.0, -1.0).astype(BF16)
    return same_c, same_s, cos8, sin8, real4, imag4, sign2


def write_table(table_ref, angle_ref, parts, odd):
    same_c, same_s, cos8, sin8, real4, imag4, sign2 = parts
    next_c, next_s = same_s, -same_c
    for t in range(BLOCK // 16):
        x, y = [], []
        for i in (2 * t, 2 * t + 1):
            c = jnp.broadcast_to(angle_ref[0, pl.ds(i, 1)], (8, BLOCK))
            s = jnp.broadcast_to(angle_ref[1, pl.ds(i, 1)], (8, BLOCK))
            x.append(c * same_c + s * same_s)
            y.append(c * next_c + s * next_s)
        x, y = jnp.concatenate(x, axis=0), jnp.concatenate(y, axis=0)
        if odd:
            x, y = x * cos8 + y * sin8, y * cos8 - x * sin8
        u, v = x.astype(BF16), y.astype(BF16)
        turned = u * real4 + v * imag4
        for step, value in ((0, u), (2, turned), (4, u * sign2), (6, turned * sign2)):
            table_ref[pl.ds((step + odd) * BLOCK + 16 * t, 16)] = value


def lag_rows(ahead, behind, tail):
    row = iota((LOCAL, 128), 0)
    lane = iota((LOCAL, 128), 1)
    ahead = jnp.where(lane <= row, tail, ahead)
    behind = jnp.where((lane >= 32) & (lane < 64 - row), tail, behind)
    reverse = 7 - iota((8, 128), 0)
    turned = []
    for at in range(0, LOCAL, 8):
        rows = jnp.take_along_axis(ahead[at : at + 8], reverse, axis=0)
        rows = pltpu.roll(rows, 120 - at, 1, stride=1, stride_axis=0)
        turned.append(jnp.take_along_axis(rows, reverse, axis=0))
    return jnp.concatenate(turned, axis=0), pltpu.roll(behind, 64, 1, stride=1, stride_axis=0)


def front_kernel(
    ahead_count, freq_count, strain_ref, ok_hbm, window_hbm, gath_ref,
    x_ref, ok_ref, window_ref, table_ref, angle_ref, spread_ref, band_ref, white_ref,
    in_sem, small_sem, send_sem, recv_sem,
):
    me = lax.axis_index("ch")
    freq = lax.axis_index("freq")
    first_bin = freq * LOCAL + 1

    small = [
        pltpu.make_async_copy(ok_hbm, ok_ref, small_sem.at[0]),
        pltpu.make_async_copy(window_hbm, window_ref, small_sem.at[1]),
    ]
    for load in small:
        load.start()
    load_strain = pltpu.make_async_copy(strain_ref, x_ref, in_sem)
    load_strain.start()

    core = me % 2
    partner = me + 1 - 2 * core
    exists = lambda other: (other >= 0) & (other < ahead_count)
    pick = lambda even, odd: jnp.where(core == 0, even, odd)
    far = pick(-3, 3)
    straight = lambda other: exists(other) & (other // RING == me // RING)
    barrier = pltpu.get_barrier_semaphore()
    peers = jnp.int32(1)
    pl.semaphore_signal(barrier, 1, device_id={"ch": partner}, device_id_type=MESH)
    for step, there in (
        (4, exists(me + 4)), (-4, exists(me - 4)), (far, straight(me + far)), (2, exists(me + 2)), (-2, exists(me - 2))
    ):
        peers = peers + there.astype(jnp.int32)

        @pl.when(there)
        def _():
            pl.semaphore_signal(barrier, 1, device_id={"ch": me + step}, device_id_type=MESH)

    parts = table_parts(angle_ref, first_bin)
    write_table(table_ref, angle_ref, parts, 0)
    write_table(table_ref, angle_ref, parts, 1)
    write_spread(spread_ref)
    write_band(band_ref, (freq > 0).astype(F32), (freq < freq_count - 1).astype(F32))

    for slot in range(10, SLOTS):
        gath_ref[slot] = jnp.zeros((TALL, 128), BF16)

    @pl.when((me < AHEAD) | (me >= ahead_count - AHEAD))
    def _():
        for distance in range(1, AHEAD + 1):
            for step, slot in ((distance, SLOT_AHEAD[distance]), (-distance, SLOT_BEHIND[distance])):

                @pl.when((me + step < 0) | (me + step >= ahead_count))
                def _():
                    gath_ref[slot] = jnp.zeros((TALL, 128), BF16)

    for load in small:
        load.wait()
    usable = (window_ref[...].astype(F32) * ok_ref[...].astype(F32)).astype(BF16)
    lane = iota((LOCAL, 128), 1)
    channel = iota((LOCAL, 128), 0)
    for slot, at in ((SLOT_AHEAD[0], channel), (SLOT_BEHIND[0], LOCAL - 1 - channel)):
        spread = jnp.dot(usable, (lane == at).astype(BF16), preferred_element_type=F32)
        gath_ref[slot, pl.ds(4 * LOCAL, WINDOWS)] = spread.astype(BF16)
    keep = []
    for half in range(2):
        expand = (iota((WINDOWS, 128), 0) == 4 * half + iota((WINDOWS, 128), 1) // 32).astype(BF16)
        keep.append(lax.dot_general(usable, expand, (((0,), (0,)), ((), ())), preferred_element_type=F32))

    load_strain.wait()
    def leveled(block):
        low = max(block * BLOCK - TIME_HALF, 0)
        high = min(block * BLOCK + BLOCK + TIME_HALF, SAMPLES)
        skip = low - (block * BLOCK - TIME_HALF)
        sums = jnp.dot(
            jnp.abs(x_ref[:, low:high]), spread_ref[skip : skip + high - low], preferred_element_type=F32
        )
        level = sums * (1.0 / (2 * TIME_HALF + 1)) + 1e-06
        return (x_ref[:, block * BLOCK : (block + 1) * BLOCK].astype(F32) / level).astype(BF16)

    spectrum = jnp.zeros((ROWS, BLOCK), F32)
    for first in (0, 2, 4, 6):
        both = jnp.concatenate([leveled(first), leveled(first + 1)], axis=1)
        spectrum = spectrum + jnp.dot(
            both, table_ref[first * BLOCK : (first + 2) * BLOCK], preferred_element_type=F32
        )
    power = spectrum * spectrum
    coarse = power.astype(BF16)
    fine = (power - coarse.astype(F32)).astype(BF16)
    smooth = jnp.dot(coarse, band_ref[...], preferred_element_type=F32) + jnp.dot(
        fine, band_ref[...], preferred_element_type=F32
    )
    white_ref[...] = spectrum[:, :128] * lax.rsqrt(smooth * (1.0 / (2 * BIN_HALF + 1)) + 1e-06)
    by_window = [white_ref[pl.ds(w, LOCAL, stride=WINDOWS)] for w in range(WINDOWS)]
    lanes = iota((LOCAL, 128), 1) // 32
    reverse = 7 - iota((8, 128), 0)
    for group in range(GROUPS):
        for half in range(2):
            piece = None
            for i in range(4):
                moved = pltpu.roll(by_window[4 * half + i], (32 * (i - group)) % 128, 1)
                piece = moved if piece is None else jnp.where(lanes == i, moved, piece)
            piece = piece * keep[half]
            where = pl.ds((2 * group + half) * LOCAL, LOCAL)
            flipped = [jnp.take_along_axis(piece[at : at + 8], reverse, axis=0) for at in range(LOCAL - 8, -1, -8)]
            gath_ref[SLOT_AHEAD[0], where] = piece.astype(BF16)
            gath_ref[SLOT_BEHIND[0], where] = jnp.concatenate(flipped, axis=0).astype(BF16)

    def copy(src, dst, which, recv, target):
        return pltpu.make_async_remote_copy(
            src_ref=gath_ref.at[src], dst_ref=gath_ref.at[dst], send_sem=send_sem.at[which],
            recv_sem=recv_sem.at[recv], device_id={"ch": target}, device_id_type=MESH,
        )

    own_sends = [
        (SLOT_BEHIND[0], SLOT_BEHIND[4], 7, me + 4, exists(me + 4)),
        (SLOT_AHEAD[0], SLOT_AHEAD[4], 3, me - 4, exists(me - 4)),
        (pick(SLOT_AHEAD[0], SLOT_BEHIND[0]), pick(SLOT_AHEAD[3], SLOT_BEHIND[3]), pick(2, 6), me + far, straight(me + far)),
        (SLOT_BEHIND[0], SLOT_BEHIND[2], 5, me + 2, exists(me + 2)),
        (SLOT_AHEAD[0], SLOT_AHEAD[2], 1, me - 2, exists(me - 2)),
        (pick(SLOT_BEHIND[0], SLOT_AHEAD[0]), pick(SLOT_BEHIND[1], SLOT_AHEAD[1]), pick(4, 0), partner, True),
    ]
    own_sends = own_sends[3:5] + own_sends[:3] + own_sends[5:]
    beyond = me + pick(4, -4)
    passes = [
        (SLOT_BEHIND[2], pick(SLOT_BEHIND[3], SLOT_BEHIND[1]), 5, pick(6, 4), exists(me - 2)),
        (SLOT_AHEAD[2], pick(SLOT_AHEAD[1], SLOT_AHEAD[3]), 1, pick(0, 2), exists(me + 2)),
        (
            pick(SLOT_AHEAD[4], SLOT_BEHIND[4]), pick(SLOT_AHEAD[3], SLOT_BEHIND[3]), pick(3, 7), pick(2, 6),
            exists(beyond) & ~straight(beyond),
        ),
    ]
    pl.semaphore_wait(barrier, peers)
    for which, (src, dst, recv, target, there) in enumerate(own_sends):
        @pl.when(there)
        def _():
            copy(src, dst, which, recv, target).start()
    for i, (src, dst, mine, recv, there) in enumerate(passes):
        @pl.when(there)
        def _():
            copy(src, src, 0, mine, partner).wait_recv()
            copy(src, dst, 6 + i, recv, partner).start()

    for slot, mine, there in (
        (pick(SLOT_AHEAD[4], SLOT_BEHIND[4]), pick(3, 7), straight(beyond)),
        (pick(SLOT_BEHIND[4], SLOT_AHEAD[4]), pick(7, 3), exists(me - pick(4, -4))),
        (pick(SLOT_AHEAD[1], SLOT_BEHIND[1]), pick(0, 4), True),
        (pick(SLOT_BEHIND[1], SLOT_AHEAD[1]), pick(4, 0), exists(me - pick(1, -1))),
        (SLOT_AHEAD[3], 2, exists(me + 3)),
        (SLOT_BEHIND[3], 6, exists(me - 3)),
    ):
        @pl.when(there)
        def _():
            copy(slot, slot, 0, mine, partner).wait_recv()
    for which, (src, dst, recv, target, there) in enumerate(own_sends):
        @pl.when(there)
        def _():
            copy(src, dst, which, recv, target).wait_send()
    for i, (src, dst, mine, recv, there) in enumerate(passes):
        @pl.when(there)
        def _():
            copy(src, dst, 6 + i, recv, partner).wait_send()


def front(strain, channel_ok, window_ok, ahead_count, freq_count):
    hbm = pl.BlockSpec(memory_space=pltpu.MemorySpace.HBM)
    vmem = pl.BlockSpec(memory_space=pltpu.VMEM)
    args = (strain.reshape(ROWS, SAMPLES), channel_ok.reshape(1, LOCAL), window_ok.T)
    return pl.pallas_call(
        functools.partial(front_kernel, ahead_count, freq_count),
        out_shape=jax.ShapeDtypeStruct((SLOTS, TALL, 128), BF16),
        in_specs=[hbm, hbm, hbm],
        out_specs=vmem,
        scratch_shapes=[
            pltpu.VMEM((ROWS, SAMPLES), BF16),
            pltpu.VMEM((1, LOCAL), jnp.int32),
            pltpu.VMEM((WINDOWS, LOCAL), jnp.int32),
            pltpu.VMEM((SAMPLES, BLOCK), BF16),
            pltpu.VMEM((2, 32, BLOCK), F32),
            pltpu.VMEM((2 * BLOCK, BLOCK), BF16),
            pltpu.VMEM((BLOCK, 128), BF16),
            pltpu.VMEM((ROWS, 128), F32),
            pltpu.SemaphoreType.DMA,
            pltpu.SemaphoreType.DMA((2,)),
            pltpu.SemaphoreType.DMA((9,)),
            pltpu.SemaphoreType.DMA((8,)),
        ],
        compiler_params=pltpu.CompilerParams(collective_id=0, has_side_effects=True, vmem_limit_bytes=VMEM_LIMIT),
        name="front",
    )(*(pltpu.with_memory_space_constraint(arg, pltpu.HBM) for arg in args))


def cross_kernel(gath_ref, ahead_hbm, behind_hbm, ahead_ref, behind_ref, out_sem):
    contract = (((1,), (1,)), ((), ()))
    per_step = LOCAL // STEPS
    use = [gath_ref[slot, pl.ds(4 * LOCAL, WINDOWS)].astype(F32) for slot in range(10)]
    beside = []
    for tile in range(3):
        moved = [pltpu.roll(use[slot], LOCAL * (slot % 4), 1) for slot in range(4 * tile, min(4 * tile + 4, 10))]
        beside.append(functools.reduce(jnp.add, moved).astype(BF16))
    pairs = lax.dot_general(
        use[0][:, :LOCAL].astype(BF16), jnp.concatenate(beside, axis=1), (((0,), (0,)), ((), ())), preferred_element_type=F32
    )
    scales = [1.0 / jnp.maximum(n, 1.0) for n in lag_rows(pairs[:, :128], pairs[:, 128:256], pairs[:, 256:])]
    lane_of = iota((LOCAL, 256), 1) % 16
    imaginary = (iota((LOCAL, 256), 1) // 16) % 2 == 1
    copies = []
    for step in range(STEPS):
        group, first = divmod(step * per_step, 16)
        low, high = (pl.ds((2 * group + half) * LOCAL, LOCAL) for half in range(2))
        own = jnp.concatenate([gath_ref[0, low], gath_ref[0, high]], axis=1)
        wide = own.astype(F32)
        swap = jnp.where(imaginary, pltpu.roll(wide, 16, 1), -pltpu.roll(wide, 240, 1)).astype(BF16)
        lhs = jnp.concatenate(
            [
                jnp.where(lane_of == first + f, value, jnp.zeros_like(value))
                for value in (own, swap)
                for f in range(per_step)
            ],
            axis=0,
        )
        rhs = jnp.concatenate([gath_ref[:, part].reshape(SLOTS * LOCAL, 128) for part in (low, high)], axis=1)
        cross = lax.dot_general(lhs, rhs, contract, preferred_element_type=F32)
        for part in range(2):
            for f in range(per_step):
                rows = slice((part * per_step + f) * LOCAL, (part * per_step + f + 1) * LOCAL)
                ahead, behind = lag_rows(cross[rows, :128], cross[rows, 128:256], cross[rows, 256:])
                ahead_ref[part, step * per_step + f] = (ahead * scales[0]).astype(BF16)
                behind_ref[part, step * per_step + f] = (behind * scales[1]).astype(BF16)
            done = pl.ds(step * per_step, per_step)
            for side, (src, dst) in enumerate(((ahead_ref, ahead_hbm), (behind_ref, behind_hbm))):
                copies.append(
                    pltpu.make_async_copy(src.at[part, done], dst.at[part, done], out_sem.at[side, part, step])
                )
                copies[-1].start()
    for copy in copies:
        copy.wait()


def cross(gathered):
    shape = (2, LOCAL, LOCAL, REACH)
    vmem = pl.BlockSpec(memory_space=pltpu.VMEM)
    hbm = pl.BlockSpec(memory_space=pltpu.MemorySpace.HBM)
    return pl.pallas_call(
        cross_kernel,
        out_shape=(jax.ShapeDtypeStruct(shape, BF16), jax.ShapeDtypeStruct(shape, BF16)),
        in_specs=[vmem],
        out_specs=(hbm, hbm),
        scratch_shapes=[pltpu.VMEM(shape, BF16), pltpu.VMEM(shape, BF16), pltpu.SemaphoreType.DMA((2, 2, STEPS))],
        compiler_params=pltpu.CompilerParams(vmem_limit_bytes=VMEM_LIMIT),
        name="cross",
    )(gathered)


def solution(mesh):
    ahead_count = mesh.shape["ch"]
    freq_count = mesh.shape["freq"]

    def per_device(strain, channel_ok, window_ok):
        gathered = front(strain, channel_ok, window_ok, ahead_count, freq_count)
        return cross(gathered)

    return jax.shard_map(
        per_device,
        mesh=mesh,
        in_specs=(P("ch", None, None), P("ch"), P("ch", None)),
        out_specs=(P(None, "freq", "ch", None), P(None, "freq", "ch", None)),
        check_vma=False,
    )
```
